32 devices in a mesh: dp: 8 (over y, x, core), fsdp: 4 (over z).
Axes of the slice: x: 2, y: 2, z: 4, core: 2. Of those that a mesh axis runs over, the one named last changes fastest.
Arguments:
- img_emb: bfloat16 [1024, 1024], P(('dp', 'fsdp')), may hold values from -0.25 to 0.25
- txt_emb: bfloat16 [1024, 1024], P(('dp', 'fsdp')), may hold values from -0.25 to 0.25
- img_ids: int32 [1024], P(('dp', 'fsdp')), may hold values from 0 to 1023
- txt_ids: int32 [1024], P(('dp', 'fsdp')), may hold values from 0 to 1023
- temp_log: float32 [1], replicated, may hold values from 1.5 to 2.5
- logit_bias: float32 [1], replicated, may hold values from -6 to -2
- block_in: bfloat16 [2048, 3072], P(('dp', 'fsdp')), may hold values from -6 to 6
- dw_kernel: float32 [49, 3072], replicated, may hold values from -0.875 to 0.875
- ln_gain: float32 [3072], replicated, may hold values from 0.5 to 1.5
- ln_bias: float32 [3072], replicated, may hold values from -3 to 3
- w_up: bfloat16 [3072, 6144], P(None, 'fsdp'), may hold values from -0.109375 to 0.109375
- w_down: bfloat16 [6144, 3072], P('fsdp'), may hold values from -0.078125 to 0.078125
- layer_scale: float32 [3072], replicated, may hold values from 0.1 to 1
- head_gain: float32 [3072], replicated, may hold values from 0.5 to 1.5
- head_bias: float32 [3072], replicated, may hold values from -3 to 3
- w_proj: bfloat16 [3072, 1024], replicated, may hold values from -0.109375 to 0.109375
Outputs:
- img_grad: float32 [1024, 1024], P(('dp', 'fsdp'))
- txt_grad: float32 [1024, 1024], P(('dp', 'fsdp'))
- w_up_grad: float32 [3072, 6144], P('dp', 'fsdp')
- w_down_grad: float32 [6144, 3072], P('fsdp', 'dp')
The draws below stay inside these ranges and needn't reach their ends.
All inputs are finite; a program needn't handle non-finite values.
Results may differ from the reference program's by a relative error of at most 0.02.
Values may be sent and summed in bfloat16 or wider, within the bound.
A program may use at most 128 MiB of HBM per device.

```python
import math
import jax
import jax.numpy as jnp
from jax import lax

WIDTH = 3072
HIDDEN_SIZE = 6144
EMBED = 1024
KERNEL = 7
SIDE = 8
PAIR_DEV = 32
PAIRS = 1024
IMAGE_ROWS = 2048
N_DP = 8
N_FSDP = 4


def set_ends(result, rng, least, top_value):
    shape = result.shape
    spot = [jax.random.randint(jax.random.fold_in(rng, axis), (), 0, shape[axis]) for axis in range(len(shape))]
    result = result.at[tuple(spot)].set(least)
    longest = shape.index(max(shape))
    spot[longest] = (spot[longest] + 1) % shape[longest]
    return result.at[tuple(spot)].set(top_value)


def block_levels(rng, dims, pieces, low, top_value):
    gain, own = 1.0, jax.random.fold_in(rng, 6)
    for dim, blocks in pieces:
        heights = jnp.exp(jax.random.uniform(jax.random.fold_in(own, dim), (blocks,), jnp.float32, low / len(pieces), top_value / len(pieces)))
        gain = gain * jnp.repeat(heights, dims[dim] // blocks).reshape([-1 if axis == dim else 1 for axis in range(len(dims))])
    return gain


def scatter_about(rng, dims, deviation, limit, cuts=(), held_as=jnp.bfloat16):
    values = deviation * jax.random.normal(rng, dims, jnp.float32)
    if cuts:
        values = values * block_levels(rng, dims, cuts, -0.22, 0.18)
    return jnp.clip(values, -limit, limit).astype(held_as)


def setup_inputs(seed: int = 0) -> dict:
    seeds = jax.random.split(jax.random.key(seed), 17)
    return {
        "img_emb": scatter_about(seeds[0], (PAIRS, EMBED), 0.03125, 0.25, ((0, 32),)),
        "txt_emb": scatter_about(seeds[1], (PAIRS, EMBED), 0.03125, 0.25, ((0, 32),)),
        "img_ids": set_ends(jax.random.randint(seeds[2], (PAIRS,), 0, PAIRS), jax.random.fold_in(seeds[2], 1), 0, PAIRS - 1).astype(jnp.int32),
        "txt_ids": set_ends(jax.random.randint(seeds[3], (PAIRS,), 0, PAIRS), jax.random.fold_in(seeds[3], 1), 0, PAIRS - 1).astype(jnp.int32),
        "temp_log": jnp.clip(jax.random.uniform(seeds[4], (1,), jnp.float32, 1.5, 2.5), 1.5, 2.5),
        "logit_bias": jnp.clip(jax.random.uniform(seeds[5], (1,), jnp.float32, -6.0, -2.0), -6.0, -2.0),
        "block_in": scatter_about(seeds[6], (IMAGE_ROWS, WIDTH), 1.0, 6.0, ((0, 32),)),
        "dw_kernel": scatter_about(seeds[7], (KERNEL * KERNEL, WIDTH), (KERNEL * KERNEL) ** -0.5, 0.875, (), jnp.float32),
        "ln_gain": jnp.clip(1.0 + 0.1 * jax.random.normal(seeds[8], (WIDTH,), jnp.float32), 0.5, 1.5),
        "ln_bias": scatter_about(seeds[9], (WIDTH,), 0.5, 3.0, (), jnp.float32),
        "w_up": scatter_about(seeds[10], (WIDTH, HIDDEN_SIZE), WIDTH ** -0.5, 0.109375, ((1, 4),)),
        "w_down": scatter_about(seeds[11], (HIDDEN_SIZE, WIDTH), HIDDEN_SIZE ** -0.5, 0.078125, ((0, 4),)),
        "layer_scale": jnp.clip(jnp.exp(jax.random.uniform(seeds[12], (WIDTH,), jnp.float32, math.log(0.1), math.log(1.0))), 0.1, 1.0),
        "head_gain": jnp.clip(1.0 + 0.1 * jax.random.normal(seeds[13], (WIDTH,), jnp.float32), 0.5, 1.5),
        "head_bias": scatter_about(seeds[14], (WIDTH,), 0.5, 3.0, (), jnp.float32),
        "w_proj": scatter_about(seeds[15], (WIDTH, EMBED), WIDTH ** -0.5, 0.109375),
    }


def unit_rows(matrix):
    values = matrix.astype(jnp.float32)
    length = jnp.sqrt(lax.optimization_barrier(jnp.sum(values * values, axis=1, keepdims=True)) + 1e-06)
    return (values / length, length)

def back_unit(gradient, unit_part, length):
    inner_prod = lax.optimization_barrier(jnp.sum(unit_part * gradient, axis=1, keepdims=True))
    return (gradient - unit_part * inner_prod) / length

def pair_tile(images, image_ids, text_rows, text_ids, temper, offset):
    scores = jnp.dot(images, text_rows.T, preferred_element_type=jnp.float32)
    logits = temper * scores + offset
    labels = jnp.where(image_ids[:, None] == text_ids[None, :], 1.0, -1.0)
    weights = (temper * -labels * jax.nn.sigmoid(-labels * logits)).astype(jnp.bfloat16)
    image_part = jnp.dot(weights, text_rows, preferred_element_type=jnp.float32)
    text_part = jnp.dot(weights.T, images, preferred_element_type=jnp.float32)
    return (image_part, text_part)

def depthwise(pictures, kernel):
    reach = KERNEL // 2
    padded = jnp.pad(pictures, ((0, 0), (reach, reach), (reach, reach), (0, 0)))
    summed = jnp.zeros_like(pictures)
    for above in range(KERNEL):
        for across in range(KERNEL):
            summed = summed + kernel[above * KERNEL + across] * padded[:, above:above + SIDE, across:across + SIDE, :]
    return summed

def layer_norm(values, gain_vec, bias_vec):
    centre = lax.optimization_barrier(jnp.mean(values, axis=-1, keepdims=True))
    centred = values - centre
    inverse = 1.0 / jnp.sqrt(lax.optimization_barrier(jnp.mean(centred * centred, axis=-1, keepdims=True)) + 1e-06)
    normal = centred * inverse
    return (normal * gain_vec + bias_vec, normal, inverse)

def head_back(patch_means, block_mean, image_sum, layer_scale, head_gain, head_bias, w_proj):
    pooled = patch_means.astype(jnp.float32) + layer_scale * block_mean
    head_out, head_norm, inverse = layer_norm(pooled, head_gain, head_bias)
    embed = jnp.dot(head_out.astype(jnp.bfloat16), w_proj, preferred_element_type=jnp.float32)
    embed_unit, embed_len = unit_rows(embed)
    embed_grad = back_unit(image_sum, embed_unit, embed_len).astype(jnp.bfloat16)
    head_grad = jnp.dot(embed_grad, w_proj.T, preferred_element_type=jnp.float32)
    norm_grad = head_grad * head_gain
    pool_grad = inverse * (norm_grad - lax.optimization_barrier(jnp.mean(norm_grad, axis=1, keepdims=True)) - head_norm * lax.optimization_barrier(jnp.mean(norm_grad * head_norm, axis=1, keepdims=True)))
    return (layer_scale * pool_grad / (SIDE * SIDE)).astype(jnp.bfloat16)

def reference(img_emb, txt_emb, img_ids, txt_ids, temp_log, logit_bias, block_in, dw_kernel, ln_gain, ln_bias, w_up, w_down, layer_scale, head_gain, head_bias, w_proj):
    temper = jnp.exp(temp_log[0])
    offset = logit_bias[0]
    img_unit, img_len = unit_rows(img_emb)
    txt_unit, txt_len = unit_rows(txt_emb)
    img_b = img_unit.astype(jnp.bfloat16)
    txt_b = txt_unit.astype(jnp.bfloat16)
    group_rows = N_FSDP * PAIR_DEV
    col_rows = N_DP * PAIR_DEV
    txt_cols = txt_b.reshape(N_DP, N_FSDP, PAIR_DEV, EMBED)
    id_cols = txt_ids.reshape(N_DP, N_FSDP, PAIR_DEV)

    def tile(running, tile_no):
        img_tot, txt_tot = running
        group_no = tile_no // N_FSDP
        column_no = tile_no % N_FSDP
        images = lax.dynamic_slice_in_dim(img_b, group_no * group_rows, group_rows, 0)
        image_ids = lax.dynamic_slice_in_dim(img_ids, group_no * group_rows, group_rows, 0)
        text_rows = lax.dynamic_index_in_dim(txt_cols, column_no, 1, keepdims=False).reshape(col_rows, EMBED)
        text_ids = lax.dynamic_index_in_dim(id_cols, column_no, 1, keepdims=False).reshape(col_rows)
        image_part, text_part = pair_tile(images, image_ids, text_rows, text_ids, temper, offset)
        image_part = lax.optimization_barrier(image_part.astype(jnp.bfloat16)).astype(jnp.float32)
        text_part = lax.optimization_barrier(text_part.astype(jnp.bfloat16)).astype(jnp.float32)
        return ((img_tot.at[group_no].add(image_part), txt_tot.at[column_no].add(text_part)), None)
    start = (jnp.zeros((N_DP, group_rows, EMBED), jnp.float32), jnp.zeros((N_FSDP, col_rows, EMBED), jnp.float32))
    (img_tot, txt_tot), _ = lax.scan(tile, start, jnp.arange(N_DP * N_FSDP, dtype=jnp.int32))
    img_sum = img_tot.reshape(PAIRS, EMBED)
    txt_sum = jnp.transpose(txt_tot.reshape(N_FSDP, N_DP, PAIR_DEV, EMBED), (1, 0, 2, 3)).reshape(PAIRS, EMBED)
    img_grad = back_unit(img_sum, img_unit, img_len)
    txt_grad = back_unit(txt_sum, txt_unit, txt_len)
    patch_rows = N_FSDP * SIDE * SIDE
    down_wide = w_down.astype(jnp.float32)

    def group_step(running, group_no):
        up_tot, down_tot = running
        patches = lax.dynamic_slice_in_dim(block_in, group_no * patch_rows, patch_rows, 0).astype(jnp.float32)
        pictures = patches.reshape(N_FSDP, SIDE, SIDE, WIDTH)
        mixed_rows = depthwise(pictures, dw_kernel).reshape(patch_rows, WIDTH)
        normed = layer_norm(mixed_rows, ln_gain, ln_bias)[0].astype(jnp.bfloat16)
        hidden = jnp.dot(normed, w_up, preferred_element_type=jnp.float32)
        active = jax.nn.gelu(hidden).astype(jnp.bfloat16)
        active_mean = lax.optimization_barrier(jnp.mean(active.astype(jnp.float32).reshape(N_FSDP, SIDE * SIDE, HIDDEN_SIZE), axis=1))
        block_mean = jnp.dot(active_mean, down_wide, precision=lax.Precision.HIGHEST)
        patch_means = lax.optimization_barrier(jnp.mean(pictures, axis=(1, 2))).astype(jnp.bfloat16)
        group_sum = lax.dynamic_slice_in_dim(img_sum, group_no * group_rows, group_rows, 0)
        micro_sum = group_sum.reshape(N_FSDP, PAIR_DEV, EMBED)[:, 0]
        grad_row = head_back(patch_means, block_mean, micro_sum, layer_scale, head_gain, head_bias, w_proj)
        out_grad = jnp.broadcast_to(grad_row[:, None, :], (N_FSDP, SIDE * SIDE, WIDTH)).reshape(patch_rows, WIDTH)
        down_grad = jnp.dot(out_grad, w_down.T, preferred_element_type=jnp.float32)
        _, pullback = jax.vjp(jax.nn.gelu, hidden)
        hid_grad = pullback(down_grad)[0].astype(jnp.bfloat16)
        down_part = jnp.dot(active.T, out_grad, preferred_element_type=jnp.float32)
        up_part = jnp.dot(normed.T, hid_grad, preferred_element_type=jnp.float32)
        up_tot = up_tot + lax.optimization_barrier(up_part.astype(jnp.bfloat16)).astype(jnp.float32)
        down_tot = down_tot + lax.optimization_barrier(down_part.astype(jnp.bfloat16)).astype(jnp.float32)
        return ((up_tot, down_tot), None)
    start = (jnp.zeros((WIDTH, HIDDEN_SIZE), jnp.float32), jnp.zeros((HIDDEN_SIZE, WIDTH), jnp.float32))
    (w_up_grad, w_down_grad), _ = lax.scan(group_step, start, jnp.arange(N_DP, dtype=jnp.int32))
    return (img_grad, txt_grad, w_up_grad, w_down_grad)
```

```python
import functools
import types

import jax
import jax.numpy as jnp
from jax import lax
from jax.experimental import pallas as pl
from jax.experimental.pallas import tpu as pltpu
from jax.sharding import PartitionSpec as P

KERNEL = 7
SIDE = 8


def unit_rows(matrix):
    values = matrix.astype(jnp.float32)
    length = jnp.sqrt(jnp.sum(values * values, axis=1, keepdims=True) + 1e-06)
    return (values / length, length)


def back_unit(gradient, unit_part, length):
    inner_prod = jnp.sum(unit_part * gradient, axis=1, keepdims=True)
    return (gradient - unit_part * inner_prod) / length


MESH = pl.DeviceIdType.MESH
VMEM = pl.BlockSpec(memory_space=pltpu.VMEM)
ANY = pl.BlockSpec(memory_space=pl.ANY)


def push(source, target, send_sem, recv_sem, **peer):
    return pltpu.make_async_remote_copy(
        src_ref=source,
        dst_ref=target,
        send_sem=send_sem,
        recv_sem=recv_sem,
        device_id=peer,
        device_id_type=MESH,
    )


def second_parts(x):
    cubic = 0.044715
    slant = 0.7978845608028654
    square = x * x
    t = jnp.tanh(slant * x * (1.0 + cubic * square))
    half = 0.5 * (1.0 + t)
    slope = half + 0.5 * x * (1.0 - t * t) * slant * (1.0 + 3.0 * cubic * square)
    return x * half, slope


def nt_dot(left, right):
    return lax.dot_general(
        left, right, (((1,), (1,)), ((), ())), preferred_element_type=jnp.float32
    )


def depthwise_norm(block, kernel, gain, bias, mixed, normed, means):
    rows, channels = block.shape
    reach = KERNEL // 2

    def tile(i, total):
        cols = pl.ds(pl.multiple_of(i * 128, 128), 128)
        grid = block[:, cols].astype(jnp.float32).reshape(SIDE, SIDE, 128)
        means[:, cols] = jnp.sum(jnp.sum(grid, axis=0), axis=0, keepdims=True) / rows
        spot = lax.broadcasted_iota(jnp.int32, (SIDE, SIDE, 128), 1)
        lines = [jnp.zeros((SIDE, 128), jnp.float32) for _ in range(SIDE)]
        for across in range(KERNEL):
            step = across - reach
            if step == 0:
                moved = grid
            else:
                moved = pltpu.roll(grid, (-step) % SIDE, axis=1)
                moved = jnp.where((spot + step >= 0) & (spot + step < SIDE), moved, 0.0)
            for above in range(KERNEL):
                k = above * KERNEL + across
                weight = jnp.broadcast_to(kernel[k : k + 1, cols], (SIDE, 128))
                for r in range(max(0, reach - above), min(SIDE, SIDE + reach - above)):
                    lines[r] = lines[r] + weight * moved[r + above - reach]
        result = jnp.concatenate(lines, axis=0)
        mixed[:, cols] = result
        return total + result

    total = lax.fori_loop(0, channels // 128, tile, jnp.zeros((rows, 128), jnp.float32))
    centre = jnp.sum(total, axis=1, keepdims=True) / channels

    def spread(i, total):
        cols = pl.ds(pl.multiple_of(i * 128, 128), 128)
        centred = mixed[:, cols] - centre
        return total + centred * centred

    total = lax.fori_loop(0, channels // 128, spread, jnp.zeros((rows, 128), jnp.float32))
    inverse = 1.0 / jnp.sqrt(jnp.sum(total, axis=1, keepdims=True) / channels + 1e-06)

    def finish(i, carry):
        cols = pl.ds(pl.multiple_of(i * 128, 128), 128)
        normal = (mixed[:, cols] - centre) * inverse
        normed[:, cols] = (normal * gain[:, cols] + bias[:, cols]).astype(normed.dtype)
        return carry

    lax.fori_loop(0, channels // 128, finish, 0)


def whole_kernel(n_dp, n_fsdp, spread, names, *refs):
    v = types.SimpleNamespace(**dict(zip(names, refs)))
    block, img_emb, txt_emb = v.block, v.img_emb, v.txt_emb
    up, down, proj, grp, gimg, ctxt = v.up, v.down, v.proj, v.grp, v.gimg, v.ctxt
    norm, slope, crit, crit_in = v.norm, v.slope, v.crit, v.crit_in
    all_slope, all_act, all_grad = v.all_slope, v.all_act, v.all_grad
    d, f = lax.axis_index("dp"), lax.axis_index("fsdp")
    rows, channels = norm.shape
    share = channels // n_dp
    embed_width = proj.shape[1]
    hid_width = up.shape[1]
    pairs = img_emb.shape[0]
    chips = n_dp // 2
    core, chip = d % 2, d // 2
    partner = d + 1 - 2 * core
    multi = chips == 4
    images = n_dp * n_fsdp

    def flip(*masks):
        return d + sum(mask - 2 * mask * ((d // mask) % 2) for mask in masks)

    loc = v.loc
    keep_up = pltpu.make_async_copy(v.up_hbm, up, loc.at[0])
    keep_down = pltpu.make_async_copy(v.down_hbm, down, loc.at[1])
    keep_proj = pltpu.make_async_copy(v.proj_hbm, proj, loc.at[2])
    keep_norm = pltpu.make_async_copy(norm, grp.at[f], loc.at[3])
    for copy in (keep_up, keep_down, keep_proj):
        copy.start()
    barrier = pltpu.get_barrier_semaphore()
    for k in range(1, n_dp):
        pl.semaphore_signal(barrier, inc=1, device_id={"dp": (d + k) % n_dp}, device_id_type=MESH)
    for k in range(1, n_fsdp):
        pl.semaphore_signal(barrier, inc=1, device_id={"fsdp": (f + k) % n_fsdp}, device_id_type=MESH)

    depthwise_norm(block, v.kernel, v.ln_gain, v.ln_bias, v.mixed, norm, v.means)
    pl.semaphore_wait(barrier, n_dp + n_fsdp - 2)

    def right(h, source, b):
        return push(source, grp.at[b], v.rgt_s.at[h], v.rgt_r.at[h], fsdp=f + 1)

    def left(h, source, b):
        return push(source, grp.at[b], v.lft_s.at[h], v.lft_r.at[h], fsdp=f - 1)

    @pl.when(f < n_fsdp - 1)
    def _():
        right(0, norm, f).start()

    @pl.when(f > 0)
    def _():
        left(0, norm, f).start()

    keep_norm.start()

    def columns(source, owner):
        return source.at[:, pl.ds(pl.multiple_of(owner * share, 128), share)]

    def column_copy(k, source, b):
        peer = (d + k) % n_dp
        return push(columns(source, peer), v.own.at[d, b], v.col_s.at[b, k - 1], v.col_r.at[b, k - 1], dp=peer)

    def column_keep(source, b):
        return pltpu.make_async_copy(columns(source, d), v.own.at[d, b], v.col_l.at[b])

    def scatter(source, b):
        if spread:
            for k in range(1, n_dp):
                column_copy(k, source, b).start()
            column_keep(source, b).start()

    def near(j, b):
        source, target = slope.at[b], all_slope.at[d, b]
        peer = flip(2 << j) if multi else (d + 2 * j + 2) % n_dp
        return push(source, target, v.slo_s.at[b, j], v.slo_r.at[b, j], dp=peer)

    def from_near(j):
        return flip(2 << j) if multi else (d - 2 * j - 2 + n_dp) % n_dp

    n_near = 2 if multi else chips - 1

    def half(j, b):
        spot = all_slope.at[flip(2 << j), b, pl.ds(j * (rows // 2), rows // 2)]
        return push(spot, spot, v.hlf_s.at[b, j], v.hlf_r.at[b, j], dp=flip(4 >> j))

    def to_partner(j, b):
        if j == 0:
            source, target = slope.at[b], all_slope.at[d, b]
        else:
            origin = flip(2, 4) if multi and j == 3 else from_near(j - 1)
            source = target = all_slope.at[origin, b]
        return push(source, target, v.par_s.at[b, j], v.par_r.at[b, j], dp=partner)

    def slope_keep(b):
        return pltpu.make_async_copy(slope.at[b], all_slope.at[d, b], v.slo_l.at[b])

    def relay(b):
        for j in range(n_near):
            near(j, b).wait_recv()
            if multi:
                half(j, b).start()
            to_partner(j + 1, b).start()

    wide = 256 if hid_width % 256 == 0 else 128

    def expand(source, b):
        def tile(i, carry):
            cols = pl.ds(pl.multiple_of(i * wide, wide), wide)
            hidden = jnp.dot(source[...], up[:, cols], preferred_element_type=jnp.float32)
            active, slant = second_parts(hidden)
            slope[b, :, cols] = slant.astype(jnp.bfloat16)
            active = active.astype(jnp.bfloat16).astype(jnp.float32)
            all_act[d, b, :, cols] = jnp.sum(active, axis=0, keepdims=True)
            return carry

        lax.fori_loop(0, hid_width // wide, tile, 0)
        for j in range(n_near):
            near(j, b).start()
        to_partner(0, b).start()
        slope_keep(b).start()

    for source, codes, spot in (
        (img_emb, v.img_codes, gimg.at[f]),
        (txt_emb, v.txt_codes, ctxt.at[d]),
    ):
        spot[:, :embed_width] = unit_rows(source[...])[0].astype(jnp.bfloat16)
        spot[:, embed_width:] = codes[...]
    img_pushes = [
        push(gimg.at[f], gimg.at[f], v.img_s.at[k - 1], v.img_r.at[k - 1], fsdp=(f + k) % n_fsdp)
        for k in range(1, n_fsdp)
    ]

    def chip_copies(ref, name):
        out = [
            push(ref.at[d], ref.at[d], getattr(v, name + "_s").at[j - 1], getattr(v, name + "_r").at[j - 1], dp=(d + 2 * j) % n_dp)
            for j in range(1, chips)
        ]
        out_near = push(ref.at[d], ref.at[d], getattr(v, name + "p_s").at[0], getattr(v, name + "p_r").at[0], dp=partner)
        onward = []
        for j in range(1, chips):
            spot = ref.at[(d + n_dp - 2 * j) % n_dp]
            onward.append(push(spot, spot, getattr(v, name + "p_s").at[j], getattr(v, name + "p_r").at[j], dp=partner))
        return out + [out_near], onward

    def forward(copies, onward):
        for copy, more in zip(copies, onward):
            copy.wait_recv()
            more.start()

    def settle(copies, onward):
        for copy in copies[: chips - 1]:
            copy.wait_send()
        copies[chips - 1].wait()
        for copy in onward:
            copy.wait()

    txt_copies, txt_onward = chip_copies(ctxt, "txt")
    for copy in img_pushes + txt_copies:
        copy.start()
    keep_up.wait()
    expand(norm, f)
    scatter(norm, f)

    def score():
        forward(txt_copies, txt_onward)
        for copy in img_pushes:
            copy.wait()
        settle(txt_copies, txt_onward)
        images_all = gimg[...].reshape(n_fsdp * pairs, -1)
        texts_all = ctxt[...].reshape(n_dp * pairs, -1)
        image_rows, image_codes = images_all[:, :embed_width], images_all[:, embed_width:]
        text_rows, text_codes = texts_all[:, :embed_width], texts_all[:, embed_width:]
        temper = jnp.exp(v.temper[...])
        offset = v.offset[...]

        def weigh(left_rows, left_codes, right_rows, right_codes):
            logits = temper * nt_dot(left_rows, right_rows) + offset
            labels = jnp.where(nt_dot(left_codes, right_codes) == 0.0, 1.0, -1.0)
            return (temper * -labels * jax.nn.sigmoid(-labels * logits)).astype(jnp.bfloat16)

        weights = weigh(image_rows, image_codes, text_rows, text_codes)
        image_part = jnp.dot(weights, text_rows, preferred_element_type=jnp.float32)
        piece = crit.shape[2]
        for p in range(n_fsdp):
            v.imgs[p] = image_part[p * pairs : (p + 1) * pairs].astype(jnp.bfloat16)
            for i in range(embed_width // piece):
                crit[p, i : i + 1, :] = image_part[p * pairs : p * pairs + 1, i * piece : (i + 1) * piece]
        weights = weigh(text_rows, text_codes, image_rows, image_codes)
        text_part = jnp.dot(weights, image_rows, preferred_element_type=jnp.float32)
        for p in range(n_dp):
            v.txts[p % 2, p // 2] = text_part[p * pairs : (p + 1) * pairs].astype(jnp.bfloat16)
        pair_copy.start()

    pair_copy = push(v.txts.at[1 - core], v.txts_pair, v.txx_s.at[0], v.txx_r.at[0], dp=partner)

    for h in range(1, n_fsdp):

        @pl.when(f - h >= 0)
        def _():
            b = f - h
            right(h - 1, norm, b).wait_recv()

            @pl.when(f < n_fsdp - 1)
            def _():
                right(h, grp.at[b], b).start()

        @pl.when(f + h <= n_fsdp - 1)
        def _():
            b = f + h
            left(h - 1, norm, b).wait_recv()

            @pl.when(f > 0)
            def _():
                left(h, grp.at[b], b).start()

        @pl.when(f - h >= 0)
        def _():
            expand(grp.at[f - h], f - h)

        @pl.when(f + h <= n_fsdp - 1)
        def _():
            expand(grp.at[f + h], f + h)

        if h == 1:
            relay(f)
        else:

            @pl.when(f - h + 1 >= 0)
            def _():
                relay(f - h + 1)

            @pl.when(f + h - 1 <= n_fsdp - 1)
            def _():
                relay(f + h - 1)

        @pl.when(f - h >= 0)
        def _():
            scatter(grp.at[f - h], f - h)

        @pl.when(f + h <= n_fsdp - 1)
        def _():
            scatter(grp.at[f + h], f + h)

        if h == 1:
            score()

    act_copies, act_onward = chip_copies(all_act, "act")
    critical, late = [], []
    for k in range(1, n_fsdp):
        peer = (f + k) % n_fsdp
        critical.append(push(crit.at[peer], crit_in.at[k - 1], v.cri_s.at[k - 1], v.cri_r.at[k - 1], fsdp=peer))
        late.append(push(v.imgs.at[peer], v.imgs_in.at[k - 1], v.ims_s.at[k - 1], v.ims_r.at[k - 1], fsdp=peer))

    totals = jnp.concatenate([all_act[d, b] for b in range(n_fsdp)], axis=0) / (SIDE * SIDE)
    high = totals.astype(jnp.bfloat16)
    low = (totals - high.astype(jnp.float32)).astype(jnp.bfloat16)
    both = jnp.concatenate([high.astype(jnp.float32), low.astype(jnp.float32)], axis=0).astype(jnp.bfloat16)
    keep_down.wait()
    partial = v.partial

    def mean_tile(i, carry):
        cols = pl.ds(pl.multiple_of(i * 256, 256), 256)
        product = jnp.dot(both, down[:, cols], preferred_element_type=jnp.float32)
        partial[:, cols] = product[:n_fsdp] + product[n_fsdp:]
        return carry

    lax.fori_loop(0, channels // 256, mean_tile, 0)
    piece = crit.shape[2]
    first = embed_width // piece
    for p in range(n_fsdp):
        for i in range(channels // piece):
            crit[p, first + i : first + i + 1, :] = partial[p : p + 1, i * piece : (i + 1) * piece]
    for copy in critical + late + act_copies:
        copy.start()

    pair_copy.wait()
    texts_own = v.txts[core].astype(jnp.float32) + v.txts_pair[...].astype(jnp.float32)
    v.txts_sum[...] = texts_own.astype(jnp.bfloat16)
    text_copies = []
    for j in range(1, chips):
        text_copies.append(
            push(
                v.txts_sum.at[(chip + j) % chips],
                v.txts_in.at[j - 1],
                v.txs_s.at[j - 1],
                v.txs_r.at[j - 1],
                dp=(d + 2 * j) % n_dp,
            )
        )
    for copy in text_copies:
        copy.start()

    for copy in critical:
        copy.wait()
    total = crit[f]
    for k in range(1, n_fsdp):
        total = total + crit_in[k - 1]
    lines = v.lines
    lines[...] = total
    image_row = jnp.concatenate([lines[i : i + 1, :] for i in range(first)], axis=1)
    block_mean = jnp.concatenate([lines[first + i : first + i + 1, :] for i in range(channels // piece)], axis=1)
    scale, gain, bias = v.scale, v.gain, v.bias
    patch_means = v.means[...].astype(jnp.bfloat16).astype(jnp.float32)
    pooled = patch_means + scale[...] * block_mean
    centred = pooled - jnp.mean(pooled, axis=1, keepdims=True)
    inverse = 1.0 / jnp.sqrt(jnp.mean(centred * centred, axis=1, keepdims=True) + 1e-06)
    head_norm = centred * inverse
    head_out = head_norm * gain[...] + bias[...]
    keep_proj.wait()
    embed = jnp.dot(
        jnp.broadcast_to(head_out, (16, channels)).astype(jnp.bfloat16),
        proj[...],
        preferred_element_type=jnp.float32,
    )[0:1]
    embed_len = jnp.sqrt(jnp.sum(embed * embed, axis=1, keepdims=True) + 1e-06)
    embed_unit = embed / embed_len
    inner_prod = jnp.sum(embed_unit * image_row, axis=1, keepdims=True)
    embed_grad = (image_row - embed_unit * inner_prod) / embed_len
    head_grad = lax.dot_general(
        jnp.broadcast_to(embed_grad, (16, embed_width)).astype(jnp.bfloat16),
        proj[...],
        (((1,), (1,)), ((), ())),
        preferred_element_type=jnp.float32,
    )[0:1]
    norm_grad = head_grad * gain[...]
    pool_grad = inverse * (
        norm_grad
        - jnp.mean(norm_grad, axis=1, keepdims=True)
        - head_norm * jnp.mean(norm_grad * head_norm, axis=1, keepdims=True)
    )
    row = scale[...] * pool_grad / (SIDE * SIDE)
    for i in range(channels // 128):
        v.grow[i : i + 1, :] = row[:, i * 128 : (i + 1) * 128]
    all_grad[d, f] = v.grow[...].astype(jnp.bfloat16)
    grads = []
    for k in range(1, n_fsdp):
        grads.append(
            push(all_grad.at[d, f], all_grad.at[d, f], v.gra_s.at[k - 1], v.gra_r.at[k - 1], fsdp=(f + k) % n_fsdp)
        )
    for copy in grads:
        copy.start()

    @pl.when(f == n_fsdp - 1)
    def _():
        relay(0)

    @pl.when(f == 0)
    def _():
        relay(n_fsdp - 1)

    for copy in grads:
        copy.wait()
    grd_copies, grd_onward = chip_copies(all_grad, "grd")
    for copy in grd_copies:
        copy.start()
    forward(act_copies, act_onward)
    forward(grd_copies, grd_onward)
    if multi:
        for b in range(n_fsdp):
            for j in range(2):
                half(j, b).wait_recv()
            to_partner(3, b).start()
    for copy in late + text_copies:
        copy.wait()
    total = v.imgs[f].astype(jnp.float32)
    for k in range(1, n_fsdp):
        total = total + v.imgs_in[k - 1].astype(jnp.float32)
    v.img_sum[...] = total
    total = v.txts[core, chip].astype(jnp.float32) + v.txts_pair[chip].astype(jnp.float32)
    for j in range(1, chips):
        total = total + v.txts_in[j - 1].astype(jnp.float32)
    v.txt_sum[...] = total
    settle(grd_copies, grd_onward)
    v.gwide[...] = all_grad[...].astype(jnp.float32).reshape(images, channels // 128, 128)
    for i in range(channels // 128):
        v.gmat[:, i * 128 : (i + 1) * 128] = v.gwide[:, i, :].astype(jnp.bfloat16)

    def down_tile(i, carry):
        spot = pl.ds(pl.multiple_of(i * wide, wide), wide)
        v.row_down[:, spot] = nt_dot(v.gmat[...], down[spot, :])
        return carry

    lax.fori_loop(0, hid_width // wide, down_tile, 0)
    settle(act_copies, act_onward)
    keep_norm.wait()
    for h in range(n_fsdp - 1):

        @pl.when((f - h >= 0) & (f < n_fsdp - 1))
        def _():
            right(h, norm, f - h).wait_send()

        @pl.when((f + h <= n_fsdp - 1) & (f > 0))
        def _():
            left(h, norm, f + h).wait_send()

    for b in range(n_fsdp):
        if spread:
            for k in range(1, n_dp):
                column_copy(k, norm, b).wait()
            column_keep(norm, b).wait()
        slope_keep(b).wait()
        for j in range(n_near):
            near(j, b).wait_send()
            if multi:
                half(j, b).wait_send()
        for j in range(chips):
            to_partner(j, b).wait()


def run_whole(n_dp, n_fsdp, args, w_up, w_down, w_proj):
    channels, embed_width = w_proj.shape
    rows = args["block"].shape[0]
    hid_width = w_up.shape[1]
    pairs = args["img_emb"].shape[0]
    share = channels // n_dp
    chips = n_dp // 2
    images = n_dp * n_fsdp
    spread = share % 128 == 0
    dma = pltpu.SemaphoreType.DMA
    f32, half = jnp.float32, jnp.bfloat16
    shape = jax.ShapeDtypeStruct
    width = embed_width + args["img_codes"].shape[1]
    piece = (channels + embed_width) // 8
    outs = dict(
        all_slope=(shape((n_dp, n_fsdp, rows, hid_width), half), ANY),
        gmat=(shape((images, channels), half), VMEM),
        row_down=(shape((images, hid_width), f32), VMEM),
        all_act=(shape((n_dp, n_fsdp, 1, hid_width), f32), VMEM),
        img_sum=(shape((pairs, embed_width), f32), VMEM),
        txt_sum=(shape((pairs, embed_width), f32), VMEM),
    )
    scratch = dict(
        up=pltpu.VMEM(w_up.shape, half),
        down=pltpu.VMEM(w_down.shape, half),
        proj=pltpu.VMEM(w_proj.shape, half),
        mixed=pltpu.VMEM((rows, channels), f32),
        norm=pltpu.VMEM((rows, channels), half),
        means=pltpu.VMEM((1, channels), f32),
        gimg=pltpu.VMEM((n_fsdp, pairs, width), half),
        ctxt=pltpu.VMEM((n_dp, pairs, width), half),
        slope=pltpu.VMEM((n_fsdp, rows, hid_width), half),
        all_grad=pltpu.VMEM((n_dp, n_fsdp, channels // 128, 128), half),
        gwide=pltpu.VMEM((images, channels // 128, 128), f32),
        grow=pltpu.VMEM((channels // 128, 128), f32),
        crit=pltpu.VMEM((n_fsdp, 8, piece), f32),
        crit_in=pltpu.VMEM((n_fsdp - 1, 8, piece), f32),
        lines=pltpu.VMEM((8, piece), f32),
        partial=pltpu.VMEM((n_fsdp, channels), f32),
        imgs=pltpu.VMEM((n_fsdp, pairs, embed_width), half),
        imgs_in=pltpu.VMEM((n_fsdp - 1, pairs, embed_width), half),
        txts=pltpu.VMEM((2, chips, pairs, embed_width), half),
        txts_pair=pltpu.VMEM((chips, pairs, embed_width), half),
        txts_sum=pltpu.VMEM((chips, pairs, embed_width), half),
        txts_in=pltpu.VMEM((chips - 1, pairs, embed_width), half),
    )
    if spread:
        outs.update(own=(shape((n_dp, n_fsdp, rows, share), half), ANY))
        scratch.update(grp=pltpu.VMEM((n_fsdp, rows, channels), half))
    else:
        outs.update(grp=(shape((n_fsdp, rows, channels), half), VMEM))
    sems = dict(
        loc=(4,),
        rgt=(n_fsdp,),
        lft=(n_fsdp,),
        col=(n_fsdp, n_dp - 1),
        slo=(n_fsdp, chips - 1),
        hlf=(n_fsdp, 2),
        par=(n_fsdp, chips),
        img=(n_fsdp - 1,),
        txt=(chips - 1,),
        txtp=(chips,),
        act=(chips - 1,),
        actp=(chips,),
        grd=(chips - 1,),
        grdp=(chips,),
        gra=(n_fsdp - 1,),
        cri=(n_fsdp - 1,),
        ims=(n_fsdp - 1,),
        txs=(chips - 1,),
        txx=(1,),
    )
    for name, dims in sems.items():
        if name == "loc":
            scratch[name] = dma(dims)
        else:
            scratch[name + "_s"] = dma(dims)
            scratch[name + "_r"] = dma(dims)
    scratch.update(col_l=dma((n_fsdp,)))
    scratch.update(slo_l=dma((n_fsdp,)))
    names = [*args, "up_hbm", "down_hbm", "proj_hbm", *outs, *scratch]
    results = pl.pallas_call(
        functools.partial(whole_kernel, n_dp, n_fsdp, spread, names),
        out_shape=[one for one, _ in outs.values()],
        in_specs=[VMEM] * len(args) + [ANY] * 3,
        out_specs=[spec for _, spec in outs.values()],
        scratch_shapes=list(scratch.values()),
        compiler_params=pltpu.CompilerParams(
            collective_id=0, has_side_effects=True, vmem_limit_bytes=60 << 20
        ),
    )(*args.values(), w_up, w_down, w_proj)
    return types.SimpleNamespace(**dict(zip(outs, results)))


def finish_kernel(
    img_emb, txt_emb, img_sum, txt_sum, act, gmat, row_down, own_hbm, slope_hbm,
    img_grad, txt_grad, up_hbm, down_hbm,
    own, own_t, slopes, hid, up, downs, sems, out_sems,
):
    tiles, all_rows, wide = slopes.shape
    images = gmat.shape[0]
    patches = all_rows // images
    share = own.shape[1]
    hid_width = tiles * wide
    own_copy = pltpu.make_async_copy(own_hbm, own, sems.at[tiles])
    own_copy.start()

    def fetch(i):
        return pltpu.make_async_copy(slope_hbm.at[:, pl.ds(i * wide, wide)], slopes.at[i], sems.at[i])

    for i in range(tiles):
        fetch(i).start()
    for source, summed, result in ((img_emb, img_sum, img_grad), (txt_emb, txt_sum, txt_grad)):
        unit_part, length = unit_rows(source[...])
        result[...] = back_unit(summed[...], unit_part, length)
    d = lax.axis_index("dp")
    own_grad = gmat[:, pl.ds(pl.multiple_of(d * share, 128), share)]
    totals = jnp.concatenate([act[i] for i in range(images)], axis=0)
    high = totals.astype(jnp.bfloat16)
    low = (totals - high.astype(jnp.float32)).astype(jnp.bfloat16)
    both = jnp.concatenate([high, low], axis=0)
    grads = jnp.concatenate([own_grad, own_grad], axis=0)
    downs[...] = lax.dot_general(both, grads, (((0,), (0,)), ((), ())), preferred_element_type=jnp.float32)
    down_out = pltpu.make_async_copy(downs, down_hbm, out_sems.at[tiles])
    down_out.start()
    own_copy.wait()
    own_t[...] = own[...].T

    def emit(i):
        return pltpu.make_async_copy(up.at[i], up_hbm.at[:, pl.ds(i * wide, wide)], out_sems.at[i])

    for i in range(tiles):
        fetch(i).wait()
        for k in range(images):
            spot = pl.ds(k * patches, patches)
            factor = row_down[k : k + 1, i * wide : (i + 1) * wide]
            hid[spot, :] = (slopes[i, spot, :].astype(jnp.float32) * factor).astype(jnp.bfloat16)
        up[i] = jnp.dot(own_t[...], hid[...], preferred_element_type=jnp.float32)
        emit(i).start()
    down_out.wait()
    for i in range(tiles):
        emit(i).wait()


def run_finish(img_emb, txt_emb, got):
    n_dp, n_fsdp, rows, share = got.own.shape
    hid_width = got.row_down.shape[1]
    images, channels = got.gmat.shape
    all_rows = images * rows
    wide = 256 if hid_width % 256 == 0 else 128
    tiles = hid_width // wide
    f32, half = jnp.float32, jnp.bfloat16
    shape = jax.ShapeDtypeStruct
    return pl.pallas_call(
        finish_kernel,
        out_shape=(
            shape(img_emb.shape, f32),
            shape(txt_emb.shape, f32),
            shape((share, hid_width), f32),
            shape((hid_width, share), f32),
        ),
        in_specs=[VMEM] * 7 + [ANY] * 2,
        out_specs=(VMEM, VMEM, ANY, ANY),
        scratch_shapes=[
            pltpu.VMEM((all_rows, share), half),
            pltpu.VMEM((share, all_rows), half),
            pltpu.VMEM((tiles, all_rows, wide), half),
            pltpu.VMEM((all_rows, wide), half),
            pltpu.VMEM((tiles, share, wide), f32),
            pltpu.VMEM((hid_width, share), f32),
            pltpu.SemaphoreType.DMA((tiles + 1,)),
            pltpu.SemaphoreType.DMA((tiles + 1,)),
        ],
        compiler_params=pltpu.CompilerParams(vmem_limit_bytes=40 << 20),
    )(
        img_emb,
        txt_emb,
        got.img_sum,
        got.txt_sum,
        got.all_act.reshape(images, 1, hid_width),
        got.gmat,
        got.row_down,
        got.own.reshape(all_rows, share),
        got.all_slope.reshape(all_rows, hid_width),
    )


def id_columns(ids, sign, flip):
    high, low, one = sign * 256 * (ids // 256), sign * (ids % 256), jnp.ones_like(ids)
    codes = [one, one, high, low] if flip else [high, low, one, one]
    return jnp.pad(jnp.stack(codes, axis=1).astype(jnp.bfloat16), ((0, 0), (0, 124)))


def split_two(values):
    high = lax.reduce_precision(values, 8, 7)
    low = values - high
    return high.astype(jnp.bfloat16), low.astype(jnp.bfloat16)


def on_device(
    img_emb,
    txt_emb,
    img_ids,
    txt_ids,
    temp_log,
    logit_bias,
    block_in,
    dw_kernel,
    ln_gain,
    ln_bias,
    w_up,
    w_down,
    layer_scale,
    head_gain,
    head_bias,
    w_proj,
):
    rows, channels = block_in.shape
    hid_width = w_up.shape[1]
    n_dp, n_fsdp = lax.axis_size("dp"), lax.axis_size("fsdp")
    args = dict(
        block=block_in,
        kernel=dw_kernel,
        ln_gain=ln_gain[None],
        ln_bias=ln_bias[None],
        img_emb=img_emb,
        txt_emb=txt_emb,
        img_codes=id_columns(img_ids, 1, False),
        txt_codes=id_columns(txt_ids, -1, True),
        temper=temp_log.reshape(1, 1),
        offset=logit_bias.reshape(1, 1),
        scale=layer_scale[None],
        gain=head_gain[None],
        bias=head_bias[None],
    )
    got = run_whole(n_dp, n_fsdp, args, w_up, w_down, w_proj)
    share = channels // n_dp
    if share % 128 == 0:
        return run_finish(img_emb, txt_emb, got)
    own_normed = lax.all_to_all(got.grp.reshape(-1, channels), "dp", split_axis=1, concat_axis=0, tiled=True)
    slopes = got.all_slope.reshape(n_dp * n_fsdp, rows, hid_width).astype(jnp.float32)
    hid_grad = (slopes * got.row_down[:, None, :]).astype(jnp.bfloat16).reshape(-1, hid_width)
    w_up_grad = lax.dot_general(
        own_normed, hid_grad, (((0,), (0,)), ((), ())), preferred_element_type=jnp.float32
    )
    own_grad = lax.dynamic_slice_in_dim(got.gmat, lax.axis_index("dp") * share, share, 1)
    high, low = split_two(got.all_act.reshape(n_dp * n_fsdp, hid_width))
    w_down_grad = lax.dot_general(
        jnp.concatenate([high, low]),
        jnp.concatenate([own_grad, own_grad]),
        (((0,), (0,)), ((), ())),
        preferred_element_type=jnp.float32,
    )
    img_unit, img_len = unit_rows(img_emb)
    txt_unit, txt_len = unit_rows(txt_emb)
    img_grad = back_unit(got.img_sum, img_unit, img_len)
    txt_grad = back_unit(got.txt_sum, txt_unit, txt_len)
    return (img_grad, txt_grad, w_up_grad, w_down_grad)


def solution(mesh):
    in_specs = (
        P(("dp", "fsdp"), None),
        P(("dp", "fsdp"), None),
        P(("dp", "fsdp")),
        P(("dp", "fsdp")),
        P(),
        P(),
        P(("dp", "fsdp"), None),
        P(),
        P(),
        P(),
        P(None, "fsdp"),
        P("fsdp", None),
        P(),
        P(),
        P(),
        P(),
    )
    out_specs = (P(("dp", "fsdp"), None), P(("dp", "fsdp"), None), P("dp", "fsdp"), P("fsdp", "dp"))
    return jax.shard_map(
        on_device, mesh=mesh, in_specs=in_specs, out_specs=out_specs, check_vma=False
    )
```

```python
import functools
import types

import jax
import jax.numpy as jnp
from jax import lax
from jax.experimental import pallas as pl
from jax.experimental.pallas import tpu as pltpu
from jax.sharding import PartitionSpec as P

KERNEL = 7
SIDE = 8


def unit_rows(matrix):
    values = matrix.astype(jnp.float32)
    length = jnp.sqrt(jnp.sum(values * values, axis=1, keepdims=True) + 1e-06)
    return (values / length, length)


def back_unit(gradient, unit_part, length):
    inner_prod = jnp.sum(unit_part * gradient, axis=1, keepdims=True)
    return (gradient - unit_part * inner_prod) / length


MESH = pl.DeviceIdType.MESH
VMEM = pl.BlockSpec(memory_space=pltpu.VMEM)
ANY = pl.BlockSpec(memory_space=pl.ANY)
HBM = pl.BlockSpec(memory_space=pltpu.HBM)


def push(source, target, send_sem, recv_sem, **peer):
    return pltpu.make_async_remote_copy(
        src_ref=source,
        dst_ref=target,
        send_sem=send_sem,
        recv_sem=recv_sem,
        device_id=peer,
        device_id_type=MESH,
    )


def second_parts(x):
    cubic = 0.044715
    slant = 0.7978845608028654
    square = x * x
    t = jnp.tanh(slant * x * (1.0 + cubic * square))
    half = 0.5 * (1.0 + t)
    slope = half + 0.5 * x * (1.0 - t * t) * slant * (1.0 + 3.0 * cubic * square)
    return x * half, slope


def nt_dot(left, right):
    return lax.dot_general(
        left, right, (((1,), (1,)), ((), ())), preferred_element_type=jnp.float32
    )


def id_codes(ids, sign, flip, width):
    pairs = ids.shape[1]
    diagonal = lax.broadcasted_iota(jnp.int32, (pairs, pairs), 0) == lax.broadcasted_iota(jnp.int32, (pairs, pairs), 1)
    spot = lax.broadcasted_iota(jnp.int32, (pairs, width), 1)

    def column(values):
        return jnp.sum(jnp.where(diagonal, (sign * values).astype(jnp.float32), 0.0), axis=1, keepdims=True)

    low = ids & 255
    first = 2 if flip else 0
    ones = (spot >= 2 - first) & (spot < 4 - first)
    codes = jnp.where(ones, 1.0, 0.0)
    codes = jnp.where(spot == first, column(ids - low), codes)
    return jnp.where(spot == first + 1, column(low), codes).astype(jnp.bfloat16)


def depthwise_norm(block, kernel, gain, bias, mixed, normed, means):
    rows, channels = block.shape
    reach = KERNEL // 2

    def tile(i, total):
        cols = pl.ds(pl.multiple_of(i * 128, 128), 128)
        grid = block[:, cols].astype(jnp.float32).reshape(SIDE, SIDE, 128)
        means[:, cols] = jnp.sum(jnp.sum(grid, axis=0), axis=0, keepdims=True) / rows
        spot = lax.broadcasted_iota(jnp.int32, (SIDE, SIDE, 128), 1)
        lines = [jnp.zeros((SIDE, 128), jnp.float32) for _ in range(SIDE)]
        for across in range(KERNEL):
            step = across - reach
            if step == 0:
                moved = grid
            else:
                moved = pltpu.roll(grid, (-step) % SIDE, axis=1)
                moved = jnp.where((spot + step >= 0) & (spot + step < SIDE), moved, 0.0)
            for above in range(KERNEL):
                k = above * KERNEL + across
                weight = jnp.broadcast_to(kernel[k : k + 1, cols], (SIDE, 128))
                for r in range(max(0, reach - above), min(SIDE, SIDE + reach - above)):
                    lines[r] = lines[r] + weight * moved[r + above - reach]
        result = jnp.concatenate(lines, axis=0)
        mixed[:, cols] = result
        return total + result

    total = lax.fori_loop(0, channels // 128, tile, jnp.zeros((rows, 128), jnp.float32))
    centre = jnp.sum(total, axis=1, keepdims=True) / channels

    def spread(i, total):
        cols = pl.ds(pl.multiple_of(i * 128, 128), 128)
        centred = mixed[:, cols] - centre
        return total + centred * centred

    total = lax.fori_loop(0, channels // 128, spread, jnp.zeros((rows, 128), jnp.float32))
    inverse = 1.0 / jnp.sqrt(jnp.sum(total, axis=1, keepdims=True) / channels + 1e-06)

    def finish(i, carry):
        cols = pl.ds(pl.multiple_of(i * 128, 128), 128)
        normal = (mixed[:, cols] - centre) * inverse
        normed[:, cols] = (normal * gain[:, cols] + bias[:, cols]).astype(normed.dtype)
        return carry

    lax.fori_loop(0, channels // 128, finish, 0)


def whole_kernel(n_dp, n_fsdp, spread, names, small, *refs):
    v = types.SimpleNamespace(**dict(zip(names, refs)))
    block, img_emb, txt_emb = v.block, v.img_emb, v.txt_emb
    up, down, proj, grp, gimg, ctxt = v.up, v.down, v.proj, v.grp, v.gimg, v.ctxt
    norm, slope, crit, crit_in = v.norm, v.slope, v.crit, v.crit_in
    all_slope, all_act, all_grad = v.all_slope, v.all_act, v.all_grad
    d, f = lax.axis_index("dp"), lax.axis_index("fsdp")
    rows, channels = norm.shape
    share = channels // n_dp
    embed_width = proj.shape[1]
    hid_width = up.shape[1]
    pairs = img_emb.shape[0]
    chips = n_dp // 2
    core, chip = d % 2, d // 2
    partner = d + 1 - 2 * core
    multi = chips == 4
    images = n_dp * n_fsdp

    def flip(*masks):
        return d + sum(mask - 2 * mask * ((d // mask) % 2) for mask in masks)

    loc = v.loc
    fetches = [
        pltpu.make_async_copy(getattr(v, name + "_hbm"), getattr(v, name), v.first.at[i])
        for i, name in enumerate(small)
    ]
    for copy in fetches:
        copy.start()
    keep_up = pltpu.make_async_copy(v.up_hbm, up, loc.at[0])
    keep_down = pltpu.make_async_copy(v.down_hbm, down, loc.at[1])
    keep_proj = pltpu.make_async_copy(v.proj_hbm, proj, loc.at[2])
    keep_norm = pltpu.make_async_copy(norm, grp.at[f], loc.at[3])
    keep_up.start()
    barrier = pltpu.get_barrier_semaphore()
    for k in range(1, n_dp):
        pl.semaphore_signal(barrier, inc=1, device_id={"dp": (d + k) % n_dp}, device_id_type=MESH)
    for k in range(1, n_fsdp):
        pl.semaphore_signal(barrier, inc=1, device_id={"fsdp": (f + k) % n_fsdp}, device_id_type=MESH)

    for copy in fetches:
        copy.wait()
    depthwise_norm(block, v.kernel, v.ln_gain, v.ln_bias, v.mixed, norm, v.means)
    pl.semaphore_wait(barrier, n_dp + n_fsdp - 2)

    def right(h, source, b):
        return push(source, grp.at[b], v.rgt_s.at[h], v.rgt_r.at[h], fsdp=f + 1)

    def left(h, source, b):
        return push(source, grp.at[b], v.lft_s.at[h], v.lft_r.at[h], fsdp=f - 1)

    @pl.when(f < n_fsdp - 1)
    def _():
        right(0, norm, f).start()

    @pl.when(f > 0)
    def _():
        left(0, norm, f).start()

    keep_norm.start()

    def columns(source, owner):
        return source.at[:, pl.ds(pl.multiple_of(owner * share, 128), share)]

    def column_copy(k, source, b):
        peer = (d + k) % n_dp
        return push(columns(source, peer), v.own.at[d, b], v.col_s.at[b, k - 1], v.col_r.at[b, k - 1], dp=peer)

    def column_keep(source, b):
        return pltpu.make_async_copy(columns(source, d), v.own.at[d, b], v.col_l.at[b])

    def scatter(source, b):
        if spread:
            for k in range(1, n_dp):
                column_copy(k, source, b).start()
            column_keep(source, b).start()

    def near(j, b):
        source, target = slope.at[b], all_slope.at[d, b]
        peer = flip(2 << j) if multi else (d + 2 * j + 2) % n_dp
        return push(source, target, v.slo_s.at[b, j], v.slo_r.at[b, j], dp=peer)

    def from_near(j):
        return flip(2 << j) if multi else (d - 2 * j - 2 + n_dp) % n_dp

    n_near = 2 if multi else chips - 1

    def half(j, b):
        spot = all_slope.at[flip(2 << j), b, pl.ds(j * (rows // 2), rows // 2)]
        return push(spot, spot, v.hlf_s.at[b, j], v.hlf_r.at[b, j], dp=flip(4 >> j))

    def to_partner(j, b):
        if j == 0:
            source, target = slope.at[b], all_slope.at[d, b]
        else:
            origin = flip(2, 4) if multi and j == 3 else from_near(j - 1)
            source = target = all_slope.at[origin, b]
        return push(source, target, v.par_s.at[b, j], v.par_r.at[b, j], dp=partner)

    def slope_keep(b):
        return pltpu.make_async_copy(slope.at[b], all_slope.at[d, b], v.slo_l.at[b])

    def relay(b):
        for j in range(n_near):
            near(j, b).wait_recv()
            if multi:
                half(j, b).start()
            to_partner(j + 1, b).start()

    wide = 256 if hid_width % 256 == 0 else 128

    def expand(source, b):
        def tile(i, carry):
            cols = pl.ds(pl.multiple_of(i * wide, wide), wide)
            hidden = jnp.dot(source[...], up[:, cols], preferred_element_type=jnp.float32)
            active, slant = second_parts(hidden)
            slope[b, :, cols] = slant.astype(jnp.bfloat16)
            active = active.astype(jnp.bfloat16).astype(jnp.float32)
            all_act[d, b, :, cols] = jnp.sum(active, axis=0, keepdims=True)
            return carry

        lax.fori_loop(0, hid_width // wide, tile, 0)
        for j in range(n_near):
            near(j, b).start()
        to_partner(0, b).start()
        slope_keep(b).start()

    for source, ids, sign, spot in (
        (img_emb, v.img_ids, 1, gimg.at[f]),
        (txt_emb, v.txt_ids, -1, ctxt.at[d]),
    ):
        spot[:, :embed_width] = unit_rows(source[...])[0].astype(jnp.bfloat16)
        spot[:, embed_width:] = id_codes(ids[...], sign, sign < 0, spot.shape[1] - embed_width)
    img_pushes = [
        push(gimg.at[f], gimg.at[f], v.img_s.at[k - 1], v.img_r.at[k - 1], fsdp=(f + k) % n_fsdp)
        for k in range(1, n_fsdp)
    ]

    def chip_copies(ref, name):
        out = [
            push(ref.at[d], ref.at[d], getattr(v, name + "_s").at[j - 1], getattr(v, name + "_r").at[j - 1], dp=(d + 2 * j) % n_dp)
            for j in range(1, chips)
        ]
        out_near = push(ref.at[d], ref.at[d], getattr(v, name + "p_s").at[0], getattr(v, name + "p_r").at[0], dp=partner)
        onward = []
        for j in range(1, chips):
            spot = ref.at[(d + n_dp - 2 * j) % n_dp]
            onward.append(push(spot, spot, getattr(v, name + "p_s").at[j], getattr(v, name + "p_r").at[j], dp=partner))
        return out + [out_near], onward

    def forward(copies, onward):
        for copy, more in zip(copies, onward):
            copy.wait_recv()
            more.start()

    def settle(copies, onward):
        for copy in copies[: chips - 1]:
            copy.wait_send()
        copies[chips - 1].wait()
        for copy in onward:
            copy.wait()

    txt_copies, txt_onward = chip_copies(ctxt, "txt")
    for copy in img_pushes + txt_copies:
        copy.start()
    keep_up.wait()
    keep_down.start()
    keep_proj.start()
    expand(norm, f)
    scatter(norm, f)

    def score():
        forward(txt_copies, txt_onward)
        for copy in img_pushes:
            copy.wait()
        settle(txt_copies, txt_onward)
        images_all = gimg[...].reshape(n_fsdp * pairs, -1)
        texts_all = ctxt[...].reshape(n_dp * pairs, -1)
        image_rows, image_codes = images_all[:, :embed_width], images_all[:, embed_width:]
        text_rows, text_codes = texts_all[:, :embed_width], texts_all[:, embed_width:]
        temper = jnp.exp(v.temper[...])
        offset = v.offset[...]

        def weigh(left_rows, left_codes, right_rows, right_codes):
            logits = temper * nt_dot(left_rows, right_rows) + offset
            labels = jnp.where(nt_dot(left_codes, right_codes) == 0.0, 1.0, -1.0)
            return (temper * -labels * jax.nn.sigmoid(-labels * logits)).astype(jnp.bfloat16)

        weights = weigh(image_rows, image_codes, text_rows, text_codes)
        image_part = jnp.dot(weights, text_rows, preferred_element_type=jnp.float32)
        piece = crit.shape[2]
        for p in range(n_fsdp):
            v.imgs[p] = image_part[p * pairs : (p + 1) * pairs].astype(jnp.bfloat16)
            for i in range(embed_width // piece):
                crit[p, i : i + 1, :] = image_part[p * pairs : p * pairs + 1, i * piece : (i + 1) * piece]
        weights = weigh(text_rows, text_codes, image_rows, image_codes)
        text_part = jnp.dot(weights, image_rows, preferred_element_type=jnp.float32)
        for p in range(n_dp):
            v.txts[p % 2, p // 2] = text_part[p * pairs : (p + 1) * pairs].astype(jnp.bfloat16)
        pair_copy.start()

    pair_copy = push(v.txts.at[1 - core], v.txts_pair, v.txx_s.at[0], v.txx_r.at[0], dp=partner)

    for h in range(1, n_fsdp):

        @pl.when(f - h >= 0)
        def _():
            b = f - h
            right(h - 1, norm, b).wait_recv()

            @pl.when(f < n_fsdp - 1)
            def _():
                right(h, grp.at[b], b).start()

        @pl.when(f + h <= n_fsdp - 1)
        def _():
            b = f + h
            left(h - 1, norm, b).wait_recv()

            @pl.when(f > 0)
            def _():
                left(h, grp.at[b], b).start()

        @pl.when(f - h >= 0)
        def _():
            expand(grp.at[f - h], f - h)

        @pl.when(f + h <= n_fsdp - 1)
        def _():
            expand(grp.at[f + h], f + h)

        if h == 1:
            relay(f)
        else:

            @pl.when(f - h + 1 >= 0)
            def _():
                relay(f - h + 1)

            @pl.when(f + h - 1 <= n_fsdp - 1)
            def _():
                relay(f + h - 1)

        if h < n_fsdp - 1:

            @pl.when(f - h >= 0)
            def _():
                scatter(grp.at[f - h], f - h)

            @pl.when(f + h <= n_fsdp - 1)
            def _():
                scatter(grp.at[f + h], f + h)

        if h == 1:
            score()

    act_copies, act_onward = chip_copies(all_act, "act")
    critical, late = [], []
    for k in range(1, n_fsdp):
        peer = (f + k) % n_fsdp
        critical.append(push(crit.at[peer], crit_in.at[k - 1], v.cri_s.at[k - 1], v.cri_r.at[k - 1], fsdp=peer))
        late.append(push(v.imgs.at[peer], v.imgs_in.at[k - 1], v.ims_s.at[k - 1], v.ims_r.at[k - 1], fsdp=peer))

    totals = jnp.concatenate([all_act[d, b] for b in range(n_fsdp)], axis=0) / (SIDE * SIDE)
    high = totals.astype(jnp.bfloat16)
    low = (totals - high.astype(jnp.float32)).astype(jnp.bfloat16)
    both = jnp.concatenate([high.astype(jnp.float32), low.astype(jnp.float32)], axis=0).astype(jnp.bfloat16)
    keep_down.wait()
    partial = v.partial

    def mean_tile(i, carry):
        cols = pl.ds(pl.multiple_of(i * 256, 256), 256)
        product = jnp.dot(both, down[:, cols], preferred_element_type=jnp.float32)
        partial[:, cols] = product[:n_fsdp] + product[n_fsdp:]
        return carry

    lax.fori_loop(0, channels // 256, mean_tile, 0)
    piece = crit.shape[2]
    first = embed_width // piece
    for p in range(n_fsdp):
        for i in range(channels // piece):
            crit[p, first + i : first + i + 1, :] = partial[p : p + 1, i * piece : (i + 1) * piece]
    for copy in critical + act_copies:
        copy.start()

    pair_copy.wait()
    texts_own = v.txts[core].astype(jnp.float32) + v.txts_pair[...].astype(jnp.float32)
    v.txts_sum[...] = texts_own.astype(jnp.bfloat16)
    text_copies = []
    for j in range(1, chips):
        text_copies.append(
            push(
                v.txts_sum.at[(chip + j) % chips],
                v.txts_in.at[j - 1],
                v.txs_s.at[j - 1],
                v.txs_r.at[j - 1],
                dp=(d + 2 * j) % n_dp,
            )
        )
    for copy in text_copies:
        copy.start()

    for copy in critical:
        copy.wait()
    total = crit[f]
    for k in range(1, n_fsdp):
        total = total + crit_in[k - 1]
    lines = v.lines
    lines[...] = total
    image_row = jnp.concatenate([lines[i : i + 1, :] for i in range(first)], axis=1)
    block_mean = jnp.concatenate([lines[first + i : first + i + 1, :] for i in range(channels // piece)], axis=1)
    scale, gain, bias = v.scale, v.gain, v.bias
    patch_means = v.means[...].astype(jnp.bfloat16).astype(jnp.float32)
    pooled = patch_means + scale[...] * block_mean
    centred = pooled - jnp.mean(pooled, axis=1, keepdims=True)
    inverse = 1.0 / jnp.sqrt(jnp.mean(centred * centred, axis=1, keepdims=True) + 1e-06)
    head_norm = centred * inverse
    head_out = head_norm * gain[...] + bias[...]
    keep_proj.wait()
    embed = jnp.dot(
        jnp.broadcast_to(head_out, (16, channels)).astype(jnp.bfloat16),
        proj[...],
        preferred_element_type=jnp.float32,
    )[0:1]
    embed_len = jnp.sqrt(jnp.sum(embed * embed, axis=1, keepdims=True) + 1e-06)
    embed_unit = embed / embed_len
    inner_prod = jnp.sum(embed_unit * image_row, axis=1, keepdims=True)
    embed_grad = (image_row - embed_unit * inner_prod) / embed_len
    head_grad = lax.dot_general(
        jnp.broadcast_to(embed_grad, (16, embed_width)).astype(jnp.bfloat16),
        proj[...],
        (((1,), (1,)), ((), ())),
        preferred_element_type=jnp.float32,
    )[0:1]
    norm_grad = head_grad * gain[...]
    pool_grad = inverse * (
        norm_grad
        - jnp.mean(norm_grad, axis=1, keepdims=True)
        - head_norm * jnp.mean(norm_grad * head_norm, axis=1, keepdims=True)
    )
    row = scale[...] * pool_grad / (SIDE * SIDE)
    for i in range(channels // 128):
        v.grow[i : i + 1, :] = row[:, i * 128 : (i + 1) * 128]
    all_grad[d, f] = v.grow[...].astype(jnp.bfloat16)
    grads = []
    for k in range(1, n_fsdp):
        grads.append(
            push(all_grad.at[d, f], all_grad.at[d, f], v.gra_s.at[k - 1], v.gra_r.at[k - 1], fsdp=(f + k) % n_fsdp)
        )
    for copy in grads + late:
        copy.start()
    for copy in grads:
        copy.wait()
    grd_copies, grd_onward = chip_copies(all_grad, "grd")
    for copy in grd_copies:
        copy.start()

    @pl.when(f == n_fsdp - 1)
    def _():
        relay(0)
        scatter(grp.at[0], 0)

    @pl.when(f == 0)
    def _():
        relay(n_fsdp - 1)
        scatter(grp.at[n_fsdp - 1], n_fsdp - 1)

    forward(grd_copies, grd_onward)
    forward(act_copies, act_onward)
    settle(grd_copies, grd_onward)
    v.gwide[...] = all_grad[...].astype(jnp.float32).reshape(images, channels // 128, 128)
    for i in range(channels // 128):
        v.gmat[:, i * 128 : (i + 1) * 128] = v.gwide[:, i, :].astype(jnp.bfloat16)

    def down_tile(i, carry):
        spot = pl.ds(pl.multiple_of(i * wide, wide), wide)
        v.row_down[:, spot] = nt_dot(v.gmat[...], down[spot, :])
        return carry

    lax.fori_loop(0, hid_width // wide, down_tile, 0)
    if multi:
        for b in range(n_fsdp):
            for j in range(2):
                half(j, b).wait_recv()
            to_partner(3, b).start()
    for copy in late + text_copies:
        copy.wait()
    total = v.imgs[f].astype(jnp.float32)
    for k in range(1, n_fsdp):
        total = total + v.imgs_in[k - 1].astype(jnp.float32)
    v.img_sum[...] = total
    total = v.txts[core, chip].astype(jnp.float32) + v.txts_pair[chip].astype(jnp.float32)
    for j in range(1, chips):
        total = total + v.txts_in[j - 1].astype(jnp.float32)
    v.txt_sum[...] = total
    settle(act_copies, act_onward)
    keep_norm.wait()
    for h in range(n_fsdp - 1):

        @pl.when((f - h >= 0) & (f < n_fsdp - 1))
        def _():
            right(h, norm, f - h).wait_send()

        @pl.when((f + h <= n_fsdp - 1) & (f > 0))
        def _():
            left(h, norm, f + h).wait_send()

    for b in range(n_fsdp):
        if spread:
            for k in range(1, n_dp):
                column_copy(k, norm, b).wait()
            column_keep(norm, b).wait()
        slope_keep(b).wait()
        for j in range(n_near):
            near(j, b).wait_send()
            if multi:
                half(j, b).wait_send()
        for j in range(chips):
            to_partner(j, b).wait()


def run_whole(n_dp, n_fsdp, args, w_up, w_down, w_proj):
    channels, embed_width = w_proj.shape
    rows = args["block"].shape[0]
    hid_width = w_up.shape[1]
    pairs = args["img_emb"].shape[0]
    share = channels // n_dp
    chips = n_dp // 2
    images = n_dp * n_fsdp
    spread = share % 128 == 0
    dma = pltpu.SemaphoreType.DMA
    f32, half = jnp.float32, jnp.bfloat16
    shape = jax.ShapeDtypeStruct
    width = embed_width + 128
    piece = (channels + embed_width) // 8
    outs = dict(
        all_slope=(shape((n_dp, n_fsdp, rows, hid_width), half), ANY),
        gmat=(shape((images, channels), half), VMEM),
        row_down=(shape((images, hid_width), f32), VMEM),
        all_act=(shape((n_dp, n_fsdp, 1, hid_width), f32), VMEM),
        img_sum=(shape((pairs, embed_width), f32), VMEM),
        txt_sum=(shape((pairs, embed_width), f32), VMEM),
    )
    scratch = dict(
        up=pltpu.VMEM(w_up.shape, half),
        down=pltpu.VMEM(w_down.shape, half),
        proj=pltpu.VMEM(w_proj.shape, half),
        mixed=pltpu.VMEM((rows, channels), f32),
        norm=pltpu.VMEM((rows, channels), half),
        means=pltpu.VMEM((1, channels), f32),
        gimg=pltpu.VMEM((n_fsdp, pairs, width), half),
        ctxt=pltpu.VMEM((n_dp, pairs, width), half),
        slope=pltpu.VMEM((n_fsdp, rows, hid_width), half),
        all_grad=pltpu.VMEM((n_dp, n_fsdp, channels // 128, 128), half),
        gwide=pltpu.VMEM((images, channels // 128, 128), f32),
        grow=pltpu.VMEM((channels // 128, 128), f32),
        crit=pltpu.VMEM((n_fsdp, 8, piece), f32),
        crit_in=pltpu.VMEM((n_fsdp - 1, 8, piece), f32),
        lines=pltpu.VMEM((8, piece), f32),
        partial=pltpu.VMEM((n_fsdp, channels), f32),
        imgs=pltpu.VMEM((n_fsdp, pairs, embed_width), half),
        imgs_in=pltpu.VMEM((n_fsdp - 1, pairs, embed_width), half),
        txts=pltpu.VMEM((2, chips, pairs, embed_width), half),
        txts_pair=pltpu.VMEM((chips, pairs, embed_width), half),
        txts_sum=pltpu.VMEM((chips, pairs, embed_width), half),
        txts_in=pltpu.VMEM((chips - 1, pairs, embed_width), half),
    )
    if spread:
        outs.update(own=(shape((n_dp, n_fsdp, rows, share), half), ANY))
        scratch.update(grp=pltpu.VMEM((n_fsdp, rows, channels), half))
    else:
        outs.update(grp=(shape((n_fsdp, rows, channels), half), VMEM))
    sems = dict(
        loc=(4,),
        rgt=(n_fsdp,),
        lft=(n_fsdp,),
        col=(n_fsdp, n_dp - 1),
        slo=(n_fsdp, chips - 1),
        hlf=(n_fsdp, 2),
        par=(n_fsdp, chips),
        img=(n_fsdp - 1,),
        txt=(chips - 1,),
        txtp=(chips,),
        act=(chips - 1,),
        actp=(chips,),
        grd=(chips - 1,),
        grdp=(chips,),
        gra=(n_fsdp - 1,),
        cri=(n_fsdp - 1,),
        ims=(n_fsdp - 1,),
        txs=(chips - 1,),
        txx=(1,),
    )
    for name, dims in sems.items():
        if name == "loc":
            scratch[name] = dma(dims)
        else:
            scratch[name + "_s"] = dma(dims)
            scratch[name + "_r"] = dma(dims)
    scratch.update(col_l=dma((n_fsdp,)))
    scratch.update(slo_l=dma((n_fsdp,)))
    for name, one in args.items():
        scratch[name] = pltpu.VMEM(one.shape, one.dtype)
    scratch.update(first=dma((len(args),)))
    inputs = [name + "_hbm" for name in [*args, "up", "down", "proj"]]
    names = [*inputs, *outs, *scratch]
    results = pl.pallas_call(
        functools.partial(whole_kernel, n_dp, n_fsdp, spread, names, list(args)),
        out_shape=[one for one, _ in outs.values()],
        in_specs=[HBM] * (len(args) + 3),
        out_specs=[spec for _, spec in outs.values()],
        scratch_shapes=list(scratch.values()),
        compiler_params=pltpu.CompilerParams(
            collective_id=0, has_side_effects=True, vmem_limit_bytes=42 << 20
        ),
    )(*[pltpu.with_memory_space_constraint(one, pltpu.HBM) if one.size > 1 else one for one in [*args.values(), w_up, w_down, w_proj]])
    return types.SimpleNamespace(**dict(zip(outs, results)))


def finish_kernel(
    img_hbm, txt_hbm, img_sum, txt_sum, act, gmat, row_down, own, slopes,
    img_grad, txt_grad, up_hbm, down_hbm,
    img_emb, txt_emb, own_t, hid, up, downs, sems, out_sems,
):
    img_copy = pltpu.make_async_copy(img_hbm, img_emb, sems.at[0])
    txt_copy = pltpu.make_async_copy(txt_hbm, txt_emb, sems.at[1])
    img_copy.start()
    txt_copy.start()
    tiles, _, wide = up.shape
    all_rows = slopes.shape[0]
    images = gmat.shape[0]
    patches = all_rows // images
    share = own.shape[1]
    hid_width = tiles * wide
    d = lax.axis_index("dp")
    own_grad = gmat[:, pl.ds(pl.multiple_of(d * share, 128), share)]
    totals = jnp.concatenate([act[i] for i in range(images)], axis=0)
    high = totals.astype(jnp.bfloat16)
    low = (totals - high.astype(jnp.float32)).astype(jnp.bfloat16)
    both = jnp.concatenate([high, low], axis=0)
    grads = jnp.concatenate([own_grad, own_grad], axis=0)
    downs[...] = lax.dot_general(both, grads, (((0,), (0,)), ((), ())), preferred_element_type=jnp.float32)
    down_out = pltpu.make_async_copy(downs, down_hbm, out_sems.at[tiles])
    down_out.start()
    own_t[...] = own[...].T
    img_copy.wait()
    txt_copy.wait()
    for source, summed, result in ((img_emb, img_sum, img_grad), (txt_emb, txt_sum, txt_grad)):
        unit_part, length = unit_rows(source[...])
        result[...] = back_unit(summed[...], unit_part, length)

    def emit(i):
        return pltpu.make_async_copy(up.at[i], up_hbm.at[:, pl.ds(i * wide, wide)], out_sems.at[i])

    def weigh(i):
        for k in range(images):
            spot = pl.ds(k * patches, patches)
            factor = row_down[k : k + 1, i * wide : (i + 1) * wide]
            hid[i % 2, spot, :] = (slopes[spot, i * wide : (i + 1) * wide].astype(jnp.float32) * factor).astype(jnp.bfloat16)

    weigh(0)
    for i in range(tiles):
        if i + 1 < tiles:
            weigh(i + 1)
        up[i] = jnp.dot(own_t[...], hid[i % 2], preferred_element_type=jnp.float32)
        emit(i).start()
    down_out.wait()
    for i in range(tiles):
        emit(i).wait()


def run_finish(img_emb, txt_emb, got):
    n_dp, n_fsdp, rows, share = got.own.shape
    hid_width = got.row_down.shape[1]
    images, channels = got.gmat.shape
    all_rows = images * rows
    wide = 256 if hid_width % 256 == 0 else 128
    tiles = hid_width // wide
    f32, half = jnp.float32, jnp.bfloat16
    shape = jax.ShapeDtypeStruct
    return pl.pallas_call(
        finish_kernel,
        out_shape=(
            shape(img_emb.shape, f32),
            shape(txt_emb.shape, f32),
            shape((share, hid_width), f32),
            shape((hid_width, share), f32),
        ),
        in_specs=[HBM] * 2 + [VMEM] * 7,
        out_specs=(VMEM, VMEM, ANY, ANY),
        scratch_shapes=[
            pltpu.VMEM(img_emb.shape, half),
            pltpu.VMEM(txt_emb.shape, half),
            pltpu.VMEM((share, all_rows), half),
            pltpu.VMEM((2, all_rows, wide), half),
            pltpu.VMEM((tiles, share, wide), f32),
            pltpu.VMEM((hid_width, share), f32),
            pltpu.SemaphoreType.DMA((2,)),
            pltpu.SemaphoreType.DMA((tiles + 1,)),
        ],
        compiler_params=pltpu.CompilerParams(vmem_limit_bytes=24 << 20),
    )(
        pltpu.with_memory_space_constraint(img_emb, pltpu.HBM),
        pltpu.with_memory_space_constraint(txt_emb, pltpu.HBM),
        got.img_sum,
        got.txt_sum,
        got.all_act.reshape(images, 1, hid_width),
        got.gmat,
        got.row_down,
        got.own.reshape(all_rows, share),
        got.all_slope.reshape(all_rows, hid_width),
    )


def split_two(values):
    high = lax.reduce_precision(values, 8, 7)
    low = values - high
    return high.astype(jnp.bfloat16), low.astype(jnp.bfloat16)


def on_device(
    img_emb,
    txt_emb,
    img_ids,
    txt_ids,
    temp_log,
    logit_bias,
    block_in,
    dw_kernel,
    ln_gain,
    ln_bias,
    w_up,
    w_down,
    layer_scale,
    head_gain,
    head_bias,
    w_proj,
):
    rows, channels = block_in.shape
    hid_width = w_up.shape[1]
    n_dp, n_fsdp = lax.axis_size("dp"), lax.axis_size("fsdp")
    args = dict(
        block=block_in,
        kernel=dw_kernel,
        ln_gain=ln_gain[None],
        ln_bias=ln_bias[None],
        img_emb=img_emb,
        txt_emb=txt_emb,
        img_ids=img_ids[None],
        txt_ids=txt_ids[None],
        temper=temp_log.reshape(1, 1),
        offset=logit_bias.reshape(1, 1),
        scale=layer_scale[None],
        gain=head_gain[None],
        bias=head_bias[None],
    )
    got = run_whole(n_dp, n_fsdp, args, w_up, w_down, w_proj)
    share = channels // n_dp
    if share % 128 == 0:
        return run_finish(img_emb, txt_emb, got)
    own_normed = lax.all_to_all(got.grp.reshape(-1, channels), "dp", split_axis=1, concat_axis=0, tiled=True)
    slopes = got.all_slope.reshape(n_dp * n_fsdp, rows, hid_width).astype(jnp.float32)
    hid_grad = (slopes * got.row_down[:, None, :]).astype(jnp.bfloat16).reshape(-1, hid_width)
    w_up_grad = lax.dot_general(
        own_normed, hid_grad, (((0,), (0,)), ((), ())), preferred_element_type=jnp.float32
    )
    own_grad = lax.dynamic_slice_in_dim(got.gmat, lax.axis_index("dp") * share, share, 1)
    high, low = split_two(got.all_act.reshape(n_dp * n_fsdp, hid_width))
    w_down_grad = lax.dot_general(
        jnp.concatenate([high, low]),
        jnp.concatenate([own_grad, own_grad]),
        (((0,), (0,)), ((), ())),
        preferred_element_type=jnp.float32,
    )
    img_unit, img_len = unit_rows(img_emb)
    txt_unit, txt_len = unit_rows(txt_emb)
    img_grad = back_unit(got.img_sum, img_unit, img_len)
    txt_grad = back_unit(got.txt_sum, txt_unit, txt_len)
    return (img_grad, txt_grad, w_up_grad, w_down_grad)


def solution(mesh):
    in_specs = (
        P(("dp", "fsdp"), None),
        P(("dp", "fsdp"), None),
        P(("dp", "fsdp")),
        P(("dp", "fsdp")),
        P(),
        P(),
        P(("dp", "fsdp"), None),
        P(),
        P(),
        P(),
        P(None, "fsdp"),
        P("fsdp", None),
        P(),
        P(),
        P(),
        P(),
    )
    out_specs = (P(("dp", "fsdp"), None), P(("dp", "fsdp"), None), P("dp", "fsdp"), P("fsdp", "dp"))
    return jax.shard_map(
        on_device, mesh=mesh, in_specs=in_specs, out_specs=out_specs, check_vma=False
    )
```

```python
import functools
import types

import jax
import jax.numpy as jnp
from jax import lax
from jax.experimental import pallas as pl
from jax.experimental.pallas import tpu as pltpu
from jax.sharding import PartitionSpec as P

KERNEL = 7
SIDE = 8


def unit_rows(matrix):
    values = matrix.astype(jnp.float32)
    length = jnp.sqrt(jnp.sum(values * values, axis=1, keepdims=True) + 1e-06)
    return (values / length, length)


def back_unit(gradient, unit_part, length):
    inner_prod = jnp.sum(unit_part * gradient, axis=1, keepdims=True)
    return (gradient - unit_part * inner_prod) / length


MESH = pl.DeviceIdType.MESH
VMEM = pl.BlockSpec(memory_space=pltpu.VMEM)
ANY = pl.BlockSpec(memory_space=pl.ANY)
HBM = pl.BlockSpec(memory_space=pltpu.HBM)


def push(source, target, send_sem, recv_sem, **peer):
    return pltpu.make_async_remote_copy(
        src_ref=source,
        dst_ref=target,
        send_sem=send_sem,
        recv_sem=recv_sem,
        device_id=peer,
        device_id_type=MESH,
    )


def second_parts(x):
    cubic = 0.044715
    slant = 0.7978845608028654
    square = x * x
    t = jnp.tanh(slant * x * (1.0 + cubic * square))
    half = 0.5 * (1.0 + t)
    slope = half + 0.5 * x * (1.0 - t * t) * slant * (1.0 + 3.0 * cubic * square)
    return x * half, slope


def nt_dot(left, right):
    return lax.dot_general(
        left, right, (((1,), (1,)), ((), ())), preferred_element_type=jnp.float32
    )


def id_codes(ids, sign, flip, width):
    pairs = ids.shape[1]
    diagonal = lax.broadcasted_iota(jnp.int32, (pairs, pairs), 0) == lax.broadcasted_iota(jnp.int32, (pairs, pairs), 1)
    spot = lax.broadcasted_iota(jnp.int32, (pairs, width), 1)

    def column(values):
        return jnp.sum(jnp.where(diagonal, (sign * values).astype(jnp.float32), 0.0), axis=1, keepdims=True)

    low = ids & 255
    first = 2 if flip else 0
    ones = (spot >= 2 - first) & (spot < 4 - first)
    codes = jnp.where(ones, 1.0, 0.0)
    codes = jnp.where(spot == first, column(ids - low), codes)
    return jnp.where(spot == first + 1, column(low), codes).astype(jnp.bfloat16)


def depthwise_norm(block, kernel, gain, bias, mixed, normed, means):
    rows, channels = block.shape
    reach = KERNEL // 2

    def tile(i, total):
        cols = pl.ds(pl.multiple_of(i * 128, 128), 128)
        grid = block[:, cols].astype(jnp.float32).reshape(SIDE, SIDE, 128)
        means[:, cols] = jnp.sum(jnp.sum(grid, axis=0), axis=0, keepdims=True) / rows
        spot = lax.broadcasted_iota(jnp.int32, (SIDE, SIDE, 128), 1)
        lines = [jnp.zeros((SIDE, 128), jnp.float32) for _ in range(SIDE)]
        for across in range(KERNEL):
            step = across - reach
            if step == 0:
                moved = grid
            else:
                moved = pltpu.roll(grid, (-step) % SIDE, axis=1)
                moved = jnp.where((spot + step >= 0) & (spot + step < SIDE), moved, 0.0)
            for above in range(KERNEL):
                k = above * KERNEL + across
                weight = jnp.broadcast_to(kernel[k : k + 1, cols], (SIDE, 128))
                for r in range(max(0, reach - above), min(SIDE, SIDE + reach - above)):
                    lines[r] = lines[r] + weight * moved[r + above - reach]
        result = jnp.concatenate(lines, axis=0)
        mixed[:, cols] = result
        return total + result

    total = lax.fori_loop(0, channels // 128, tile, jnp.zeros((rows, 128), jnp.float32))
    centre = jnp.sum(total, axis=1, keepdims=True) / channels

    def spread(i, total):
        cols = pl.ds(pl.multiple_of(i * 128, 128), 128)
        centred = mixed[:, cols] - centre
        return total + centred * centred

    total = lax.fori_loop(0, channels // 128, spread, jnp.zeros((rows, 128), jnp.float32))
    inverse = 1.0 / jnp.sqrt(jnp.sum(total, axis=1, keepdims=True) / channels + 1e-06)

    def finish(i, carry):
        cols = pl.ds(pl.multiple_of(i * 128, 128), 128)
        normal = (mixed[:, cols] - centre) * inverse
        normed[:, cols] = (normal * gain[:, cols] + bias[:, cols]).astype(normed.dtype)
        return carry

    lax.fori_loop(0, channels // 128, finish, 0)


def whole_kernel(n_dp, n_fsdp, spread, names, small, *refs):
    v = types.SimpleNamespace(**dict(zip(names, refs)))
    block, img_emb, txt_emb = v.block, v.img_emb, v.txt_emb
    up, down, proj, grp, gimg, ctxt = v.up, v.down, v.proj, v.grp, v.gimg, v.ctxt
    norm, slope, crit, crit_in = v.norm, v.slope, v.crit, v.crit_in
    all_slope, all_act, all_grad = v.all_slope, v.all_act, v.all_grad
    d, f = lax.axis_index("dp"), lax.axis_index("fsdp")
    rows, channels = norm.shape
    share = channels // n_dp
    embed_width = proj.shape[1]
    hid_width = up.shape[1]
    pairs = img_emb.shape[0]
    chips = n_dp // 2
    core, chip = d % 2, d // 2
    partner = d + 1 - 2 * core
    multi = chips == 4
    images = n_dp * n_fsdp

    def flip(*masks):
        return d + sum(mask - 2 * mask * ((d // mask) % 2) for mask in masks)

    loc = v.loc
    fetches = [
        pltpu.make_async_copy(getattr(v, name + "_hbm"), getattr(v, name), v.first.at[i])
        for i, name in enumerate(small)
    ]
    for copy in fetches:
        copy.start()
    keep_up = pltpu.make_async_copy(v.up_hbm, up, loc.at[0])
    keep_down = pltpu.make_async_copy(v.down_hbm, down, loc.at[1])
    keep_proj = pltpu.make_async_copy(v.proj_hbm, proj, loc.at[2])
    keep_norm = pltpu.make_async_copy(norm, grp.at[f], loc.at[3])
    keep_up.start()
    barrier = pltpu.get_barrier_semaphore()
    for k in range(1, n_dp):
        pl.semaphore_signal(barrier, inc=1, device_id={"dp": (d + k) % n_dp}, device_id_type=MESH)
    for k in range(1, n_fsdp):
        pl.semaphore_signal(barrier, inc=1, device_id={"fsdp": (f + k) % n_fsdp}, device_id_type=MESH)

    for copy in fetches:
        copy.wait()
    depthwise_norm(block, v.kernel, v.ln_gain, v.ln_bias, v.mixed, norm, v.means)
    pl.semaphore_wait(barrier, n_dp + n_fsdp - 2)

    def right(h, source, b):
        return push(source, grp.at[b], v.rgt_s.at[h], v.rgt_r.at[h], fsdp=f + 1)

    def left(h, source, b):
        return push(source, grp.at[b], v.lft_s.at[h], v.lft_r.at[h], fsdp=f - 1)

    @pl.when(f < n_fsdp - 1)
    def _():
        right(0, norm, f).start()

    @pl.when(f > 0)
    def _():
        left(0, norm, f).start()

    keep_norm.start()

    def columns(source, owner):
        return source.at[:, pl.ds(pl.multiple_of(owner * share, 128), share)]

    def column_copy(k, source, b):
        peer = (d + k) % n_dp
        return push(columns(source, peer), v.own.at[d, b], v.col_s.at[b, k - 1], v.col_r.at[b, k - 1], dp=peer)

    def column_keep(source, b):
        return pltpu.make_async_copy(columns(source, d), v.own.at[d, b], v.col_l.at[b])

    def scatter(source, b):
        if spread:
            for k in range(1, n_dp):
                column_copy(k, source, b).start()
            column_keep(source, b).start()

    def near(j, b):
        source, target = slope.at[b], all_slope.at[d, b]
        peer = flip(2 << j) if multi else (d + 2 * j + 2) % n_dp
        return push(source, target, v.slo_s.at[b, j], v.slo_r.at[b, j], dp=peer)

    def from_near(j):
        return flip(2 << j) if multi else (d - 2 * j - 2 + n_dp) % n_dp

    n_near = 2 if multi else chips - 1

    def half(j, b):
        spot = all_slope.at[flip(2 << j), b, pl.ds(j * (rows // 2), rows // 2)]
        return push(spot, spot, v.hlf_s.at[b, j], v.hlf_r.at[b, j], dp=flip(4 >> j))

    def to_partner(j, b):
        if j == 0:
            source, target = slope.at[b], all_slope.at[d, b]
        else:
            origin = flip(2, 4) if multi and j == 3 else from_near(j - 1)
            source = target = all_slope.at[origin, b]
        return push(source, target, v.par_s.at[b, j], v.par_r.at[b, j], dp=partner)

    def slope_keep(b):
        return pltpu.make_async_copy(slope.at[b], all_slope.at[d, b], v.slo_l.at[b])

    def relay(b):
        for j in range(n_near):
            near(j, b).wait_recv()
            if multi:
                half(j, b).start()
            to_partner(j + 1, b).start()

    wide = 256 if hid_width % 256 == 0 else 128

    def expand(source, b):
        def tile(i, carry):
            cols = pl.ds(pl.multiple_of(i * wide, wide), wide)
            hidden = jnp.dot(source[...], up[:, cols], preferred_element_type=jnp.float32)
            active, slant = second_parts(hidden)
            slope[b, :, cols] = slant.astype(jnp.bfloat16)
            active = active.astype(jnp.bfloat16).astype(jnp.float32)
            all_act[d, b, :, cols] = jnp.sum(active, axis=0, keepdims=True)
            return carry

        lax.fori_loop(0, hid_width // wide, tile, 0)
        for j in range(n_near):
            near(j, b).start()
        to_partner(0, b).start()
        slope_keep(b).start()

    for source, ids, sign, spot in (
        (img_emb, v.img_ids, 1, gimg.at[f]),
        (txt_emb, v.txt_ids, -1, ctxt.at[d]),
    ):
        spot[:, :embed_width] = unit_rows(source[...])[0].astype(jnp.bfloat16)
        spot[:, embed_width:] = id_codes(ids[...], sign, sign < 0, spot.shape[1] - embed_width)
    img_pushes = [
        push(gimg.at[f], gimg.at[f], v.img_s.at[k - 1], v.img_r.at[k - 1], fsdp=(f + k) % n_fsdp)
        for k in range(1, n_fsdp)
    ]

    def chip_copies(ref, name):
        out = [
            push(ref.at[d], ref.at[d], getattr(v, name + "_s").at[j - 1], getattr(v, name + "_r").at[j - 1], dp=(d + 2 * j) % n_dp)
            for j in range(1, chips)
        ]
        out_near = push(ref.at[d], ref.at[d], getattr(v, name + "p_s").at[0], getattr(v, name + "p_r").at[0], dp=partner)
        onward = []
        for j in range(1, chips):
            spot = ref.at[(d + n_dp - 2 * j) % n_dp]
            onward.append(push(spot, spot, getattr(v, name + "p_s").at[j], getattr(v, name + "p_r").at[j], dp=partner))
        return out + [out_near], onward

    def forward(copies, onward):
        for copy, more in zip(copies, onward):
            copy.wait_recv()
            more.start()

    def settle(copies, onward):
        for copy in copies[: chips - 1]:
            copy.wait_send()
        copies[chips - 1].wait()
        for copy in onward:
            copy.wait()

    txt_copies, txt_onward = chip_copies(ctxt, "txt")
    for copy in txt_copies:
        copy.start()
    keep_up.wait()
    keep_down.start()
    keep_proj.start()
    expand(norm, f)
    scatter(norm, f)

    def score():
        forward(txt_copies, txt_onward)
        for copy in img_pushes:
            copy.wait()
        settle(txt_copies, txt_onward)
        images_all = gimg[...].reshape(n_fsdp * pairs, -1)
        texts_all = ctxt[...].reshape(n_dp * pairs, -1)
        image_rows, image_codes = images_all[:, :embed_width], images_all[:, embed_width:]
        text_rows, text_codes = texts_all[:, :embed_width], texts_all[:, embed_width:]
        temper = jnp.exp(v.temper[...])
        offset = v.offset[...]

        def weigh(left_rows, left_codes, right_rows, right_codes):
            logits = temper * nt_dot(left_rows, right_rows) + offset
            labels = jnp.where(nt_dot(left_codes, right_codes) == 0.0, 1.0, -1.0)
            return (temper * -labels * jax.nn.sigmoid(-labels * logits)).astype(jnp.bfloat16)

        weights = weigh(image_rows, image_codes, text_rows, text_codes)
        image_part = jnp.dot(weights, text_rows, preferred_element_type=jnp.float32)
        piece = crit.shape[2]
        for p in range(n_fsdp):
            v.imgs[p] = image_part[p * pairs : (p + 1) * pairs].astype(jnp.bfloat16)
            for i in range(embed_width // piece):
                crit[p, i : i + 1, :] = image_part[p * pairs : p * pairs + 1, i * piece : (i + 1) * piece]
        weights = weigh(text_rows, text_codes, image_rows, image_codes)
        text_part = jnp.dot(weights, image_rows, preferred_element_type=jnp.float32)
        for p in range(n_dp):
            v.txts[p % 2, p // 2] = text_part[p * pairs : (p + 1) * pairs].astype(jnp.bfloat16)
        pair_copy.start()

    pair_copy = push(v.txts.at[1 - core], v.txts_pair, v.txx_s.at[0], v.txx_r.at[0], dp=partner)

    for h in range(1, n_fsdp):

        @pl.when(f - h >= 0)
        def _():
            b = f - h
            right(h - 1, norm, b).wait_recv()

            @pl.when(f < n_fsdp - 1)
            def _():
                right(h, grp.at[b], b).start()

        @pl.when(f + h <= n_fsdp - 1)
        def _():
            b = f + h
            left(h - 1, norm, b).wait_recv()

            @pl.when(f > 0)
            def _():
                left(h, grp.at[b], b).start()

        if h == 1:
            for copy in img_pushes:
                copy.start()

        @pl.when(f - h >= 0)
        def _():
            expand(grp.at[f - h], f - h)

        @pl.when(f + h <= n_fsdp - 1)
        def _():
            expand(grp.at[f + h], f + h)

        if h == 1:
            relay(f)
        else:

            @pl.when(f - h + 1 >= 0)
            def _():
                relay(f - h + 1)

            @pl.when(f + h - 1 <= n_fsdp - 1)
            def _():
                relay(f + h - 1)

        if h < n_fsdp - 1:

            @pl.when(f - h >= 0)
            def _():
                scatter(grp.at[f - h], f - h)

            @pl.when(f + h <= n_fsdp - 1)
            def _():
                scatter(grp.at[f + h], f + h)

        if h == min(2, n_fsdp - 1):
            score()

    act_copies, act_onward = chip_copies(all_act, "act")
    critical, late = [], []
    for k in range(1, n_fsdp):
        peer = (f + k) % n_fsdp
        critical.append(push(crit.at[peer], crit_in.at[k - 1], v.cri_s.at[k - 1], v.cri_r.at[k - 1], fsdp=peer))
        late.append(push(v.imgs.at[peer], v.imgs_in.at[k - 1], v.ims_s.at[k - 1], v.ims_r.at[k - 1], fsdp=peer))

    totals = jnp.concatenate([all_act[d, b] for b in range(n_fsdp)], axis=0) / (SIDE * SIDE)
    high = totals.astype(jnp.bfloat16)
    low = (totals - high.astype(jnp.float32)).astype(jnp.bfloat16)
    both = jnp.concatenate([high.astype(jnp.float32), low.astype(jnp.float32)], axis=0).astype(jnp.bfloat16)
    keep_down.wait()
    partial = v.partial

    def mean_tile(i, carry):
        cols = pl.ds(pl.multiple_of(i * 256, 256), 256)
        product = jnp.dot(both, down[:, cols], preferred_element_type=jnp.float32)
        partial[:, cols] = product[:n_fsdp] + product[n_fsdp:]
        return carry

    lax.fori_loop(0, channels // 256, mean_tile, 0)
    piece = crit.shape[2]
    first = embed_width // piece
    for p in range(n_fsdp):
        for i in range(channels // piece):
            crit[p, first + i : first + i + 1, :] = partial[p : p + 1, i * piece : (i + 1) * piece]
    for copy in critical + act_copies:
        copy.start()

    pair_copy.wait()
    texts_own = v.txts[core].astype(jnp.float32) + v.txts_pair[...].astype(jnp.float32)
    v.txts_sum[...] = texts_own.astype(jnp.bfloat16)
    text_copies = []
    for j in range(1, chips):
        text_copies.append(
            push(
                v.txts_sum.at[(chip + j) % chips],
                v.txts_in.at[j - 1],
                v.txs_s.at[j - 1],
                v.txs_r.at[j - 1],
                dp=(d + 2 * j) % n_dp,
            )
        )
    for copy in text_copies:
        copy.start()

    for copy in critical:
        copy.wait()
    total = crit[f]
    for k in range(1, n_fsdp):
        total = total + crit_in[k - 1]
    lines = v.lines
    lines[...] = total
    image_row = jnp.concatenate([lines[i : i + 1, :] for i in range(first)], axis=1)
    block_mean = jnp.concatenate([lines[first + i : first + i + 1, :] for i in range(channels // piece)], axis=1)
    scale, gain, bias = v.scale, v.gain, v.bias
    patch_means = v.means[...].astype(jnp.bfloat16).astype(jnp.float32)
    pooled = patch_means + scale[...] * block_mean
    centred = pooled - jnp.mean(pooled, axis=1, keepdims=True)
    inverse = 1.0 / jnp.sqrt(jnp.mean(centred * centred, axis=1, keepdims=True) + 1e-06)
    head_norm = centred * inverse
    head_out = head_norm * gain[...] + bias[...]
    keep_proj.wait()
    embed = jnp.dot(
        jnp.broadcast_to(head_out, (16, channels)).astype(jnp.bfloat16),
        proj[...],
        preferred_element_type=jnp.float32,
    )[0:1]
    embed_len = jnp.sqrt(jnp.sum(embed * embed, axis=1, keepdims=True) + 1e-06)
    embed_unit = embed / embed_len
    inner_prod = jnp.sum(embed_unit * image_row, axis=1, keepdims=True)
    embed_grad = (image_row - embed_unit * inner_prod) / embed_len
    head_grad = lax.dot_general(
        jnp.broadcast_to(embed_grad, (16, embed_width)).astype(jnp.bfloat16),
        proj[...],
        (((1,), (1,)), ((), ())),
        preferred_element_type=jnp.float32,
    )[0:1]
    norm_grad = head_grad * gain[...]
    pool_grad = inverse * (
        norm_grad
        - jnp.mean(norm_grad, axis=1, keepdims=True)
        - head_norm * jnp.mean(norm_grad * head_norm, axis=1, keepdims=True)
    )
    row = scale[...] * pool_grad / (SIDE * SIDE)
    for i in range(channels // 128):
        v.grow[i : i + 1, :] = row[:, i * 128 : (i + 1) * 128]
    all_grad[d, f] = v.grow[...].astype(jnp.bfloat16)
    grads = []
    for k in range(1, n_fsdp):
        grads.append(
            push(all_grad.at[d, f], all_grad.at[d, f], v.gra_s.at[k - 1], v.gra_r.at[k - 1], fsdp=(f + k) % n_fsdp)
        )
    for copy in grads + late:
        copy.start()
    for copy in grads:
        copy.wait()
    grd_copies, grd_onward = chip_copies(all_grad, "grd")
    for copy in grd_copies:
        copy.start()

    @pl.when(f == n_fsdp - 1)
    def _():
        relay(0)
        scatter(grp.at[0], 0)

    @pl.when(f == 0)
    def _():
        relay(n_fsdp - 1)
        scatter(grp.at[n_fsdp - 1], n_fsdp - 1)

    def diagonal(b):
        for j in range(2):
            half(j, b).wait_recv()
        to_partner(3, b).start()

    forward(grd_copies, grd_onward)
    forward(act_copies, act_onward)
    settle(grd_copies, grd_onward)
    if multi:
        for b in range(n_fsdp):

            @pl.when(((f != n_fsdp - 1) | (b != 0)) & ((f != 0) | (b != n_fsdp - 1)))
            def _():
                diagonal(b)

    v.gwide[...] = all_grad[...].astype(jnp.float32).reshape(images, channels // 128, 128)
    for i in range(channels // 128):
        v.gmat[:, i * 128 : (i + 1) * 128] = v.gwide[:, i, :].astype(jnp.bfloat16)

    def down_tile(i, carry):
        spot = pl.ds(pl.multiple_of(i * wide, wide), wide)
        v.row_down[:, spot] = nt_dot(v.gmat[...], down[spot, :])
        return carry

    lax.fori_loop(0, hid_width // wide, down_tile, 0)
    if multi:

        @pl.when(f == n_fsdp - 1)
        def _():
            diagonal(0)

        @pl.when(f == 0)
        def _():
            diagonal(n_fsdp - 1)

    for copy in late + text_copies:
        copy.wait()
    total = v.imgs[f].astype(jnp.float32)
    for k in range(1, n_fsdp):
        total = total + v.imgs_in[k - 1].astype(jnp.float32)
    v.img_sum[...] = total
    total = v.txts[core, chip].astype(jnp.float32) + v.txts_pair[chip].astype(jnp.float32)
    for j in range(1, chips):
        total = total + v.txts_in[j - 1].astype(jnp.float32)
    v.txt_sum[...] = total
    settle(act_copies, act_onward)
    keep_norm.wait()
    for h in range(n_fsdp - 1):

        @pl.when((f - h >= 0) & (f < n_fsdp - 1))
        def _():
            right(h, norm, f - h).wait_send()

        @pl.when((f + h <= n_fsdp - 1) & (f > 0))
        def _():
            left(h, norm, f + h).wait_send()

    for b in range(n_fsdp):
        if spread:
            for k in range(1, n_dp):
                column_copy(k, norm, b).wait()
            column_keep(norm, b).wait()
        slope_keep(b).wait()
        for j in range(n_near):
            near(j, b).wait_send()
            if multi:
                half(j, b).wait_send()
        for j in range(chips):
            to_partner(j, b).wait()


def run_whole(n_dp, n_fsdp, args, w_up, w_down, w_proj):
    channels, embed_width = w_proj.shape
    rows = args["block"].shape[0]
    hid_width = w_up.shape[1]
    pairs = args["img_emb"].shape[0]
    share = channels // n_dp
    chips = n_dp // 2
    images = n_dp * n_fsdp
    spread = share % 128 == 0
    dma = pltpu.SemaphoreType.DMA
    f32, half = jnp.float32, jnp.bfloat16
    shape = jax.ShapeDtypeStruct
    width = embed_width + 128
    piece = (channels + embed_width) // 8
    outs = dict(
        all_slope=(shape((n_dp, n_fsdp, rows, hid_width), half), ANY),
        gmat=(shape((images, channels), half), VMEM),
        row_down=(shape((images, hid_width), f32), VMEM),
        all_act=(shape((n_dp, n_fsdp, 1, hid_width), f32), VMEM),
        img_sum=(shape((pairs, embed_width), f32), VMEM),
        txt_sum=(shape((pairs, embed_width), f32), VMEM),
    )
    scratch = dict(
        up=pltpu.VMEM(w_up.shape, half),
        down=pltpu.VMEM(w_down.shape, half),
        proj=pltpu.VMEM(w_proj.shape, half),
        mixed=pltpu.VMEM((rows, channels), f32),
        norm=pltpu.VMEM((rows, channels), half),
        means=pltpu.VMEM((1, channels), f32),
        gimg=pltpu.VMEM((n_fsdp, pairs, width), half),
        ctxt=pltpu.VMEM((n_dp, pairs, width), half),
        slope=pltpu.VMEM((n_fsdp, rows, hid_width), half),
        all_grad=pltpu.VMEM((n_dp, n_fsdp, channels // 128, 128), half),
        gwide=pltpu.VMEM((images, channels // 128, 128), f32),
        grow=pltpu.VMEM((channels // 128, 128), f32),
        crit=pltpu.VMEM((n_fsdp, 8, piece), f32),
        crit_in=pltpu.VMEM((n_fsdp - 1, 8, piece), f32),
        lines=pltpu.VMEM((8, piece), f32),
        partial=pltpu.VMEM((n_fsdp, channels), f32),
        imgs=pltpu.VMEM((n_fsdp, pairs, embed_width), half),
        imgs_in=pltpu.VMEM((n_fsdp - 1, pairs, embed_width), half),
        txts=pltpu.VMEM((2, chips, pairs, embed_width), half),
        txts_pair=pltpu.VMEM((chips, pairs, embed_width), half),
        txts_sum=pltpu.VMEM((chips, pairs, embed_width), half),
        txts_in=pltpu.VMEM((chips - 1, pairs, embed_width), half),
    )
    if spread:
        outs.update(own=(shape((n_dp, n_fsdp, rows, share), half), ANY))
        scratch.update(grp=pltpu.VMEM((n_fsdp, rows, channels), half))
    else:
        outs.update(grp=(shape((n_fsdp, rows, channels), half), VMEM))
    sems = dict(
        loc=(4,),
        rgt=(n_fsdp,),
        lft=(n_fsdp,),
        col=(n_fsdp, n_dp - 1),
        slo=(n_fsdp, chips - 1),
        hlf=(n_fsdp, 2),
        par=(n_fsdp, chips),
        img=(n_fsdp - 1,),
        txt=(chips - 1,),
        txtp=(chips,),
        act=(chips - 1,),
        actp=(chips,),
        grd=(chips - 1,),
        grdp=(chips,),
        gra=(n_fsdp - 1,),
        cri=(n_fsdp - 1,),
        ims=(n_fsdp - 1,),
        txs=(chips - 1,),
        txx=(1,),
    )
    for name, dims in sems.items():
        if name == "loc":
            scratch[name] = dma(dims)
        else:
            scratch[name + "_s"] = dma(dims)
            scratch[name + "_r"] = dma(dims)
    scratch.update(col_l=dma((n_fsdp,)))
    scratch.update(slo_l=dma((n_fsdp,)))
    for name, one in args.items():
        scratch[name] = pltpu.VMEM(one.shape, one.dtype)
    scratch.update(first=dma((len(args),)))
    inputs = [name + "_hbm" for name in [*args, "up", "down", "proj"]]
    names = [*inputs, *outs, *scratch]
    results = pl.pallas_call(
        functools.partial(whole_kernel, n_dp, n_fsdp, spread, names, list(args)),
        out_shape=[one for one, _ in outs.values()],
        in_specs=[HBM] * (len(args) + 3),
        out_specs=[spec for _, spec in outs.values()],
        scratch_shapes=list(scratch.values()),
        compiler_params=pltpu.CompilerParams(
            collective_id=0, has_side_effects=True, vmem_limit_bytes=42 << 20
        ),
    )(*[pltpu.with_memory_space_constraint(one, pltpu.HBM) if one.size > 1 else one for one in [*args.values(), w_up, w_down, w_proj]])
    return types.SimpleNamespace(**dict(zip(outs, results)))


def finish_kernel(
    img_hbm, txt_hbm, img_sum, txt_sum, act, gmat, row_down, own, slopes,
    img_grad, txt_grad, up_hbm, down_hbm,
    img_emb, txt_emb, own_t, hid, up, downs, sems, out_sems,
):
    img_copy = pltpu.make_async_copy(img_hbm, img_emb, sems.at[0])
    txt_copy = pltpu.make_async_copy(txt_hbm, txt_emb, sems.at[1])
    img_copy.start()
    txt_copy.start()
    tiles, _, wide = up.shape
    all_rows = slopes.shape[0]
    images = gmat.shape[0]
    patches = all_rows // images
    share = own.shape[1]
    hid_width = tiles * wide
    d = lax.axis_index("dp")
    own_grad = gmat[:, pl.ds(pl.multiple_of(d * share, 128), share)]
    totals = jnp.concatenate([act[i] for i in range(images)], axis=0)
    high = totals.astype(jnp.bfloat16)
    low = (totals - high.astype(jnp.float32)).astype(jnp.bfloat16)
    both = jnp.concatenate([high, low], axis=0)
    grads = jnp.concatenate([own_grad, own_grad], axis=0)
    downs[...] = lax.dot_general(both, grads, (((0,), (0,)), ((), ())), preferred_element_type=jnp.float32)
    down_out = pltpu.make_async_copy(downs, down_hbm, out_sems.at[tiles])
    down_out.start()
    own_t[...] = own[...].T
    img_copy.wait()
    txt_copy.wait()
    for source, summed, result in ((img_emb, img_sum, img_grad), (txt_emb, txt_sum, txt_grad)):
        unit_part, length = unit_rows(source[...])
        result[...] = back_unit(summed[...], unit_part, length)

    def emit(i):
        return pltpu.make_async_copy(up.at[i], up_hbm.at[:, pl.ds(i * wide, wide)], out_sems.at[i])

    def weigh(i):
        for k in range(images):
            spot = pl.ds(k * patches, patches)
            factor = row_down[k : k + 1, i * wide : (i + 1) * wide]
            hid[i % 2, spot, :] = (slopes[spot, i * wide : (i + 1) * wide].astype(jnp.float32) * factor).astype(jnp.bfloat16)

    weigh(0)
    for i in range(tiles):
        if i + 1 < tiles:
            weigh(i + 1)
        up[i] = jnp.dot(own_t[...], hid[i % 2], preferred_element_type=jnp.float32)
        emit(i).start()
    down_out.wait()
    for i in range(tiles):
        emit(i).wait()


def run_finish(img_emb, txt_emb, got):
    n_dp, n_fsdp, rows, share = got.own.shape
    hid_width = got.row_down.shape[1]
    images, channels = got.gmat.shape
    all_rows = images * rows
    wide = 256 if hid_width % 256 == 0 else 128
    tiles = hid_width // wide
    f32, half = jnp.float32, jnp.bfloat16
    shape = jax.ShapeDtypeStruct
    return pl.pallas_call(
        finish_kernel,
        out_shape=(
            shape(img_emb.shape, f32),
            shape(txt_emb.shape, f32),
            shape((share, hid_width), f32),
            shape((hid_width, share), f32),
        ),
        in_specs=[HBM] * 2 + [VMEM] * 7,
        out_specs=(VMEM, VMEM, ANY, ANY),
        scratch_shapes=[
            pltpu.VMEM(img_emb.shape, half),
            pltpu.VMEM(txt_emb.shape, half),
            pltpu.VMEM((share, all_rows), half),
            pltpu.VMEM((2, all_rows, wide), half),
            pltpu.VMEM((tiles, share, wide), f32),
            pltpu.VMEM((hid_width, share), f32),
            pltpu.SemaphoreType.DMA((2,)),
            pltpu.SemaphoreType.DMA((tiles + 1,)),
        ],
        compiler_params=pltpu.CompilerParams(vmem_limit_bytes=24 << 20),
    )(
        pltpu.with_memory_space_constraint(img_emb, pltpu.HBM),
        pltpu.with_memory_space_constraint(txt_emb, pltpu.HBM),
        got.img_sum,
        got.txt_sum,
        got.all_act.reshape(images, 1, hid_width),
        got.gmat,
        got.row_down,
        got.own.reshape(all_rows, share),
        got.all_slope.reshape(all_rows, hid_width),
    )


def split_two(values):
    high = lax.reduce_precision(values, 8, 7)
    low = values - high
    return high.astype(jnp.bfloat16), low.astype(jnp.bfloat16)


def on_device(
    img_emb,
    txt_emb,
    img_ids,
    txt_ids,
    temp_log,
    logit_bias,
    block_in,
    dw_kernel,
    ln_gain,
    ln_bias,
    w_up,
    w_down,
    layer_scale,
    head_gain,
    head_bias,
    w_proj,
):
    rows, channels = block_in.shape
    hid_width = w_up.shape[1]
    n_dp, n_fsdp = lax.axis_size("dp"), lax.axis_size("fsdp")
    args = dict(
        block=block_in,
        kernel=dw_kernel,
        ln_gain=ln_gain[None],
        ln_bias=ln_bias[None],
        img_emb=img_emb,
        txt_emb=txt_emb,
        img_ids=img_ids[None],
        txt_ids=txt_ids[None],
        temper=temp_log.reshape(1, 1),
        offset=logit_bias.reshape(1, 1),
        scale=layer_scale[None],
        gain=head_gain[None],
        bias=head_bias[None],
    )
    got = run_whole(n_dp, n_fsdp, args, w_up, w_down, w_proj)
    share = channels // n_dp
    if share % 128 == 0:
        return run_finish(img_emb, txt_emb, got)
    own_normed = lax.all_to_all(got.grp.reshape(-1, channels), "dp", split_axis=1, concat_axis=0, tiled=True)
    slopes = got.all_slope.reshape(n_dp * n_fsdp, rows, hid_width).astype(jnp.float32)
    hid_grad = (slopes * got.row_down[:, None, :]).astype(jnp.bfloat16).reshape(-1, hid_width)
    w_up_grad = lax.dot_general(
        own_normed, hid_grad, (((0,), (0,)), ((), ())), preferred_element_type=jnp.float32
    )
    own_grad = lax.dynamic_slice_in_dim(got.gmat, lax.axis_index("dp") * share, share, 1)
    high, low = split_two(got.all_act.reshape(n_dp * n_fsdp, hid_width))
    w_down_grad = lax.dot_general(
        jnp.concatenate([high, low]),
        jnp.concatenate([own_grad, own_grad]),
        (((0,), (0,)), ((), ())),
        preferred_element_type=jnp.float32,
    )
    img_unit, img_len = unit_rows(img_emb)
    txt_unit, txt_len = unit_rows(txt_emb)
    img_grad = back_unit(got.img_sum, img_unit, img_len)
    txt_grad = back_unit(got.txt_sum, txt_unit, txt_len)
    return (img_grad, txt_grad, w_up_grad, w_down_grad)


def solution(mesh):
    in_specs = (
        P(("dp", "fsdp"), None),
        P(("dp", "fsdp"), None),
        P(("dp", "fsdp")),
        P(("dp", "fsdp")),
        P(),
        P(),
        P(("dp", "fsdp"), None),
        P(),
        P(),
        P(),
        P(None, "fsdp"),
        P("fsdp", None),
        P(),
        P(),
        P(),
        P(),
    )
    out_specs = (P(("dp", "fsdp"), None), P(("dp", "fsdp"), None), P("dp", "fsdp"), P("fsdp", "dp"))
    return jax.shard_map(
        on_device, mesh=mesh, in_specs=in_specs, out_specs=out_specs, check_vma=False
    )
```

```python
import functools
import types

import jax
import jax.numpy as jnp
from jax import lax
from jax.experimental import pallas as pl
from jax.experimental.pallas import tpu as pltpu
from jax.sharding import PartitionSpec as P

KERNEL = 7
SIDE = 8


def unit_rows(matrix):
    values = matrix.astype(jnp.float32)
    length = jnp.sqrt(jnp.sum(values * values, axis=1, keepdims=True) + 1e-06)
    return (values / length, length)


def back_unit(gradient, unit_part, length):
    inner_prod = jnp.sum(unit_part * gradient, axis=1, keepdims=True)
    return (gradient - unit_part * inner_prod) / length


MESH = pl.DeviceIdType.MESH
VMEM = pl.BlockSpec(memory_space=pltpu.VMEM)
ANY = pl.BlockSpec(memory_space=pl.ANY)
HBM = pl.BlockSpec(memory_space=pltpu.HBM)


def push(source, target, send_sem, recv_sem, **peer):
    return pltpu.make_async_remote_copy(
        src_ref=source,
        dst_ref=target,
        send_sem=send_sem,
        recv_sem=recv_sem,
        device_id=peer,
        device_id_type=MESH,
    )


def second_parts(x):
    cubic = 0.044715
    slant = 0.7978845608028654
    square = x * x
    t = jnp.tanh(slant * x * (1.0 + cubic * square))
    half = 0.5 * (1.0 + t)
    slope = half + 0.5 * x * (1.0 - t * t) * slant * (1.0 + 3.0 * cubic * square)
    return x * half, slope


def nt_dot(left, right):
    return lax.dot_general(
        left, right, (((1,), (1,)), ((), ())), preferred_element_type=jnp.float32
    )


def id_codes(ids, sign, flip, width):
    pairs = ids.shape[1]
    diagonal = lax.broadcasted_iota(jnp.int32, (pairs, pairs), 0) == lax.broadcasted_iota(jnp.int32, (pairs, pairs), 1)
    spot = lax.broadcasted_iota(jnp.int32, (pairs, width), 1)

    def column(values):
        return jnp.sum(jnp.where(diagonal, (sign * values).astype(jnp.float32), 0.0), axis=1, keepdims=True)

    low = ids & 255
    first = 2 if flip else 0
    ones = (spot >= 2 - first) & (spot < 4 - first)
    codes = jnp.where(ones, 1.0, 0.0)
    codes = jnp.where(spot == first, column(ids - low), codes)
    return jnp.where(spot == first + 1, column(low), codes).astype(jnp.bfloat16)


def depthwise_norm(block, kernel, gain, bias, mixed, normed, means):
    rows, channels = block.shape
    reach = KERNEL // 2

    def tile(i, total):
        cols = pl.ds(pl.multiple_of(i * 128, 128), 128)
        grid = block[:, cols].astype(jnp.float32).reshape(SIDE, SIDE, 128)
        means[:, cols] = jnp.sum(jnp.sum(grid, axis=0), axis=0, keepdims=True) / rows
        spot = lax.broadcasted_iota(jnp.int32, (SIDE, SIDE, 128), 1)
        lines = [jnp.zeros((SIDE, 128), jnp.float32) for _ in range(SIDE)]
        for across in range(KERNEL):
            step = across - reach
            if step == 0:
                moved = grid
            else:
                moved = pltpu.roll(grid, (-step) % SIDE, axis=1)
                moved = jnp.where((spot + step >= 0) & (spot + step < SIDE), moved, 0.0)
            for above in range(KERNEL):
                k = above * KERNEL + across
                weight = jnp.broadcast_to(kernel[k : k + 1, cols], (SIDE, 128))
                for r in range(max(0, reach - above), min(SIDE, SIDE + reach - above)):
                    lines[r] = lines[r] + weight * moved[r + above - reach]
        result = jnp.concatenate(lines, axis=0)
        mixed[:, cols] = result
        return total + result

    total = lax.fori_loop(0, channels // 128, tile, jnp.zeros((rows, 128), jnp.float32))
    centre = jnp.sum(total, axis=1, keepdims=True) / channels

    def spread(i, total):
        cols = pl.ds(pl.multiple_of(i * 128, 128), 128)
        centred = mixed[:, cols] - centre
        return total + centred * centred

    total = lax.fori_loop(0, channels // 128, spread, jnp.zeros((rows, 128), jnp.float32))
    inverse = 1.0 / jnp.sqrt(jnp.sum(total, axis=1, keepdims=True) / channels + 1e-06)

    def finish(i, carry):
        cols = pl.ds(pl.multiple_of(i * 128, 128), 128)
        normal = (mixed[:, cols] - centre) * inverse
        normed[:, cols] = (normal * gain[:, cols] + bias[:, cols]).astype(normed.dtype)
        return carry

    lax.fori_loop(0, channels // 128, finish, 0)


def whole_kernel(n_dp, n_fsdp, spread, names, small, *refs):
    v = types.SimpleNamespace(**dict(zip(names, refs)))
    block, img_emb, txt_emb = v.block, v.img_emb, v.txt_emb
    up, down, proj, grp, gimg, ctxt = v.up, v.down, v.proj, v.grp, v.gimg, v.ctxt
    norm, slope, crit, crit_in = v.norm, v.slope, v.crit, v.crit_in
    all_slope, all_act, all_grad = v.all_slope, v.all_act, v.all_grad
    d, f = lax.axis_index("dp"), lax.axis_index("fsdp")
    rows, channels = norm.shape
    share = channels // n_dp
    embed_width = proj.shape[1]
    hid_width = up.shape[1]
    pairs = img_emb.shape[0]
    chips = n_dp // 2
    core, chip = d % 2, d // 2
    partner = d + 1 - 2 * core
    multi = chips == 4
    images = n_dp * n_fsdp

    def flip(*masks):
        return d + sum(mask - 2 * mask * ((d // mask) % 2) for mask in masks)

    loc = v.loc
    fetches = [
        pltpu.make_async_copy(getattr(v, name + "_hbm"), getattr(v, name), v.first.at[i])
        for i, name in enumerate(small)
    ]
    for copy in fetches:
        copy.start()
    keep_up = pltpu.make_async_copy(v.up_hbm, up, loc.at[0])
    keep_down = pltpu.make_async_copy(v.down_hbm, down, loc.at[1])
    keep_proj = pltpu.make_async_copy(v.proj_hbm, proj, loc.at[2])
    keep_norm = pltpu.make_async_copy(norm, grp.at[f], loc.at[3])
    keep_up.start()
    barrier = pltpu.get_barrier_semaphore()
    for k in range(1, n_dp):
        pl.semaphore_signal(barrier, inc=1, device_id={"dp": (d + k) % n_dp}, device_id_type=MESH)
    for k in range(1, n_fsdp):
        pl.semaphore_signal(barrier, inc=1, device_id={"fsdp": (f + k) % n_fsdp}, device_id_type=MESH)

    for copy in fetches:
        copy.wait()
    depthwise_norm(block, v.kernel, v.ln_gain, v.ln_bias, v.mixed, norm, v.means)
    pl.semaphore_wait(barrier, n_dp + n_fsdp - 2)

    def right(h, source, b):
        return push(source, grp.at[b], v.rgt_s.at[h], v.rgt_r.at[h], fsdp=f + 1)

    def left(h, source, b):
        return push(source, grp.at[b], v.lft_s.at[h], v.lft_r.at[h], fsdp=f - 1)

    @pl.when(f < n_fsdp - 1)
    def _():
        right(0, norm, f).start()

    @pl.when(f > 0)
    def _():
        left(0, norm, f).start()

    keep_norm.start()

    def columns(source, owner):
        return source.at[:, pl.ds(pl.multiple_of(owner * share, 128), share)]

    def column_copy(k, source, b):
        peer = (d + k) % n_dp
        return push(columns(source, peer), v.own.at[d, b], v.col_s.at[b, k - 1], v.col_r.at[b, k - 1], dp=peer)

    def column_keep(source, b):
        return pltpu.make_async_copy(columns(source, d), v.own.at[d, b], v.col_l.at[b])

    def scatter(source, b):
        if spread:
            for k in range(1, n_dp):
                column_copy(k, source, b).start()
            column_keep(source, b).start()

    def near(j, b):
        source, target = slope.at[b], all_slope.at[d, b]
        peer = flip(2 << j) if multi else (d + 2 * j + 2) % n_dp
        return push(source, target, v.slo_s.at[b, j], v.slo_r.at[b, j], dp=peer)

    def from_near(j):
        return flip(2 << j) if multi else (d - 2 * j - 2 + n_dp) % n_dp

    n_near = 2 if multi else chips - 1

    def half(j, b):
        spot = all_slope.at[flip(2 << j), b, pl.ds(j * (rows // 2), rows // 2)]
        return push(spot, spot, v.hlf_s.at[b, j], v.hlf_r.at[b, j], dp=flip(4 >> j))

    def to_partner(j, b):
        if j == 0:
            source, target = slope.at[b], all_slope.at[d, b]
        else:
            origin = flip(2, 4) if multi and j == 3 else from_near(j - 1)
            source = target = all_slope.at[origin, b]
        return push(source, target, v.par_s.at[b, j], v.par_r.at[b, j], dp=partner)

    def slope_keep(b):
        return pltpu.make_async_copy(slope.at[b], all_slope.at[d, b], v.slo_l.at[b])

    def relay(b):
        for j in range(n_near):
            near(j, b).wait_recv()
            if multi:
                half(j, b).start()
            to_partner(j + 1, b).start()

    wide = 256 if hid_width % 256 == 0 else 128

    def expand(source, b):
        def tile(i, carry):
            cols = pl.ds(pl.multiple_of(i * wide, wide), wide)
            hidden = jnp.dot(source[...], up[:, cols], preferred_element_type=jnp.float32)
            active, slant = second_parts(hidden)
            slope[b, :, cols] = slant.astype(jnp.bfloat16)
            active = active.astype(jnp.bfloat16).astype(jnp.float32)
            all_act[d, b, :, cols] = jnp.sum(active, axis=0, keepdims=True)
            return carry

        lax.fori_loop(0, hid_width // wide, tile, 0)
        for j in range(n_near):
            near(j, b).start()
        to_partner(0, b).start()
        slope_keep(b).start()

    for source, ids, sign, spot in (
        (img_emb, v.img_ids, 1, gimg.at[f]),
        (txt_emb, v.txt_ids, -1, ctxt.at[d]),
    ):
        spot[:, :embed_width] = unit_rows(source[...])[0].astype(jnp.bfloat16)
        spot[:, embed_width:] = id_codes(ids[...], sign, sign < 0, spot.shape[1] - embed_width)
    img_pushes = [
        push(gimg.at[f], gimg.at[f], v.img_s.at[k - 1], v.img_r.at[k - 1], fsdp=(f + k) % n_fsdp)
        for k in range(1, n_fsdp)
    ]

    def chip_copies(ref, name):
        out = [
            push(ref.at[d], ref.at[d], getattr(v, name + "_s").at[j - 1], getattr(v, name + "_r").at[j - 1], dp=(d + 2 * j) % n_dp)
            for j in range(1, chips)
        ]
        out_near = push(ref.at[d], ref.at[d], getattr(v, name + "p_s").at[0], getattr(v, name + "p_r").at[0], dp=partner)
        onward = []
        for j in range(1, chips):
            spot = ref.at[(d + n_dp - 2 * j) % n_dp]
            onward.append(push(spot, spot, getattr(v, name + "p_s").at[j], getattr(v, name + "p_r").at[j], dp=partner))
        return out + [out_near], onward

    def forward(copies, onward):
        for copy, more in zip(copies, onward):
            copy.wait_recv()
            more.start()

    def settle(copies, onward):
        for copy in copies[: chips - 1]:
            copy.wait_send()
        copies[chips - 1].wait()
        for copy in onward:
            copy.wait()

    txt_copies, txt_onward = chip_copies(ctxt, "txt")
    for copy in txt_copies:
        copy.start()
    keep_up.wait()
    keep_down.start()
    keep_proj.start()
    expand(norm, f)
    scatter(norm, f)

    def score():
        forward(txt_copies, txt_onward)
        for copy in img_pushes:
            copy.wait()
        settle(txt_copies, txt_onward)
        images_all = gimg[...].reshape(n_fsdp * pairs, -1)
        texts_all = ctxt[...].reshape(n_dp * pairs, -1)
        image_rows, image_codes = images_all[:, :embed_width], images_all[:, embed_width:]
        text_rows, text_codes = texts_all[:, :embed_width], texts_all[:, embed_width:]
        temper = jnp.exp(v.temper[...])
        offset = v.offset[...]

        def weigh(left_rows, left_codes, right_rows, right_codes):
            logits = temper * nt_dot(left_rows, right_rows) + offset
            labels = jnp.where(nt_dot(left_codes, right_codes) == 0.0, 1.0, -1.0)
            return (temper * -labels * jax.nn.sigmoid(-labels * logits)).astype(jnp.bfloat16)

        weights = weigh(image_rows, image_codes, text_rows, text_codes)
        image_part = jnp.dot(weights, text_rows, preferred_element_type=jnp.float32)
        piece = crit.shape[2]
        for p in range(n_fsdp):
            v.imgs[p] = image_part[p * pairs : (p + 1) * pairs].astype(jnp.bfloat16)
            for i in range(embed_width // piece):
                crit[p, i : i + 1, :] = image_part[p * pairs : p * pairs + 1, i * piece : (i + 1) * piece]
        weights = weigh(text_rows, text_codes, image_rows, image_codes)
        text_part = jnp.dot(weights, image_rows, preferred_element_type=jnp.float32)
        for p in range(n_dp):
            v.txts[p % 2, p // 2] = text_part[p * pairs : (p + 1) * pairs].astype(jnp.bfloat16)
        pair_copy.start()

    pair_copy = push(v.txts.at[1 - core], v.txts_pair, v.txx_s.at[0], v.txx_r.at[0], dp=partner)

    for h in range(1, n_fsdp):

        @pl.when(f - h >= 0)
        def _():
            b = f - h
            right(h - 1, norm, b).wait_recv()

            @pl.when(f < n_fsdp - 1)
            def _():
                right(h, grp.at[b], b).start()

        @pl.when(f + h <= n_fsdp - 1)
        def _():
            b = f + h
            left(h - 1, norm, b).wait_recv()

            @pl.when(f > 0)
            def _():
                left(h, grp.at[b], b).start()

        if h == 1:
            for copy in img_pushes:
                copy.start()

        @pl.when(f - h >= 0)
        def _():
            expand(grp.at[f - h], f - h)

        @pl.when(f + h <= n_fsdp - 1)
        def _():
            expand(grp.at[f + h], f + h)

        if h == 1:
            relay(f)
        else:

            @pl.when(f - h + 1 >= 0)
            def _():
                relay(f - h + 1)

            @pl.when(f + h - 1 <= n_fsdp - 1)
            def _():
                relay(f + h - 1)

        if h < n_fsdp - 1:

            @pl.when(f - h >= 0)
            def _():
                scatter(grp.at[f - h], f - h)

            @pl.when(f + h <= n_fsdp - 1)
            def _():
                scatter(grp.at[f + h], f + h)

        if h == min(2, n_fsdp - 1):
            score()

    act_copies, act_onward = chip_copies(all_act, "act")
    critical, late = [], []
    for k in range(1, n_fsdp):
        peer = (f + k) % n_fsdp
        critical.append(push(crit.at[peer], crit_in.at[k - 1], v.cri_s.at[k - 1], v.cri_r.at[k - 1], fsdp=peer))
        late.append(push(v.imgs.at[peer], v.imgs_in.at[k - 1], v.ims_s.at[k - 1], v.ims_r.at[k - 1], fsdp=peer))

    totals = jnp.concatenate([all_act[d, b] for b in range(n_fsdp)], axis=0) / (SIDE * SIDE)
    high = totals.astype(jnp.bfloat16)
    low = (totals - high.astype(jnp.float32)).astype(jnp.bfloat16)
    both = jnp.concatenate([high.astype(jnp.float32), low.astype(jnp.float32)], axis=0).astype(jnp.bfloat16)
    keep_down.wait()
    partial = v.partial

    def mean_tile(i, carry):
        cols = pl.ds(pl.multiple_of(i * 256, 256), 256)
        product = jnp.dot(both, down[:, cols], preferred_element_type=jnp.float32)
        partial[:, cols] = product[:n_fsdp] + product[n_fsdp:]
        return carry

    lax.fori_loop(0, channels // 256, mean_tile, 0)
    piece = crit.shape[2]
    first = embed_width // piece
    for p in range(n_fsdp):
        for i in range(channels // piece):
            crit[p, first + i : first + i + 1, :] = partial[p : p + 1, i * piece : (i + 1) * piece]
    for copy in critical:
        copy.start()

    pair_copy.wait()
    texts_own = v.txts[core].astype(jnp.float32) + v.txts_pair[...].astype(jnp.float32)
    v.txts_sum[...] = texts_own.astype(jnp.bfloat16)
    text_copies = []
    for j in range(1, chips):
        text_copies.append(
            push(
                v.txts_sum.at[(chip + j) % chips],
                v.txts_in.at[j - 1],
                v.txs_s.at[j - 1],
                v.txs_r.at[j - 1],
                dp=(d + 2 * j) % n_dp,
            )
        )

    for copy in critical:
        copy.wait()
    total = crit[f]
    for k in range(1, n_fsdp):
        total = total + crit_in[k - 1]
    lines = v.lines
    lines[...] = total
    image_row = jnp.concatenate([lines[i : i + 1, :] for i in range(first)], axis=1)
    block_mean = jnp.concatenate([lines[first + i : first + i + 1, :] for i in range(channels // piece)], axis=1)
    scale, gain, bias = v.scale, v.gain, v.bias
    patch_means = v.means[...].astype(jnp.bfloat16).astype(jnp.float32)
    pooled = patch_means + scale[...] * block_mean
    centred = pooled - jnp.mean(pooled, axis=1, keepdims=True)
    inverse = 1.0 / jnp.sqrt(jnp.mean(centred * centred, axis=1, keepdims=True) + 1e-06)
    head_norm = centred * inverse
    head_out = head_norm * gain[...] + bias[...]
    keep_proj.wait()
    embed = jnp.dot(
        jnp.broadcast_to(head_out, (16, channels)).astype(jnp.bfloat16),
        proj[...],
        preferred_element_type=jnp.float32,
    )[0:1]
    embed_len = jnp.sqrt(jnp.sum(embed * embed, axis=1, keepdims=True) + 1e-06)
    embed_unit = embed / embed_len
    inner_prod = jnp.sum(embed_unit * image_row, axis=1, keepdims=True)
    embed_grad = (image_row - embed_unit * inner_prod) / embed_len
    head_grad = lax.dot_general(
        jnp.broadcast_to(embed_grad, (16, embed_width)).astype(jnp.bfloat16),
        proj[...],
        (((1,), (1,)), ((), ())),
        preferred_element_type=jnp.float32,
    )[0:1]
    norm_grad = head_grad * gain[...]
    pool_grad = inverse * (
        norm_grad
        - jnp.mean(norm_grad, axis=1, keepdims=True)
        - head_norm * jnp.mean(norm_grad * head_norm, axis=1, keepdims=True)
    )
    row = scale[...] * pool_grad / (SIDE * SIDE)
    for i in range(channels // 128):
        v.grow[i : i + 1, :] = row[:, i * 128 : (i + 1) * 128]
    all_grad[d, f] = v.grow[...].astype(jnp.bfloat16)
    grads = []
    for k in range(1, n_fsdp):
        grads.append(
            push(all_grad.at[d, f], all_grad.at[d, f], v.gra_s.at[k - 1], v.gra_r.at[k - 1], fsdp=(f + k) % n_fsdp)
        )
    for copy in grads + late:
        copy.start()
    for copy in grads:
        copy.wait()
    grd_copies, grd_onward = chip_copies(all_grad, "grd")
    for copy in grd_copies + act_copies + text_copies:
        copy.start()

    @pl.when(f == n_fsdp - 1)
    def _():
        relay(0)
        scatter(grp.at[0], 0)

    @pl.when(f == 0)
    def _():
        relay(n_fsdp - 1)
        scatter(grp.at[n_fsdp - 1], n_fsdp - 1)

    def diagonal(b):
        for j in range(2):
            half(j, b).wait_recv()
        to_partner(3, b).start()

    forward(grd_copies, grd_onward)
    settle(grd_copies, grd_onward)
    if multi:
        for b in range(n_fsdp):

            @pl.when(((f != n_fsdp - 1) | (b != 0)) & ((f != 0) | (b != n_fsdp - 1)))
            def _():
                diagonal(b)

    v.gwide[...] = all_grad[...].astype(jnp.float32).reshape(images, channels // 128, 128)
    for i in range(channels // 128):
        v.gmat[:, i * 128 : (i + 1) * 128] = v.gwide[:, i, :].astype(jnp.bfloat16)

    def down_tile(i, carry):
        spot = pl.ds(pl.multiple_of(i * wide, wide), wide)
        v.row_down[:, spot] = nt_dot(v.gmat[...], down[spot, :])
        return carry

    lax.fori_loop(0, hid_width // wide, down_tile, 0)
    forward(act_copies, act_onward)
    if multi:

        @pl.when(f == n_fsdp - 1)
        def _():
            diagonal(0)

        @pl.when(f == 0)
        def _():
            diagonal(n_fsdp - 1)

    for copy in late + text_copies:
        copy.wait()
    total = v.imgs[f].astype(jnp.float32)
    for k in range(1, n_fsdp):
        total = total + v.imgs_in[k - 1].astype(jnp.float32)
    v.img_sum[...] = total
    total = v.txts[core, chip].astype(jnp.float32) + v.txts_pair[chip].astype(jnp.float32)
    for j in range(1, chips):
        total = total + v.txts_in[j - 1].astype(jnp.float32)
    v.txt_sum[...] = total
    settle(act_copies, act_onward)
    keep_norm.wait()
    for h in range(n_fsdp - 1):

        @pl.when((f - h >= 0) & (f < n_fsdp - 1))
        def _():
            right(h, norm, f - h).wait_send()

        @pl.when((f + h <= n_fsdp - 1) & (f > 0))
        def _():
            left(h, norm, f + h).wait_send()

    for b in range(n_fsdp):
        if spread:
            for k in range(1, n_dp):
                column_copy(k, norm, b).wait()
            column_keep(norm, b).wait()
        slope_keep(b).wait()
        for j in range(n_near):
            near(j, b).wait_send()
            if multi:
                half(j, b).wait_send()
        for j in range(chips):
            to_partner(j, b).wait()


def run_whole(n_dp, n_fsdp, args, w_up, w_down, w_proj):
    channels, embed_width = w_proj.shape
    rows = args["block"].shape[0]
    hid_width = w_up.shape[1]
    pairs = args["img_emb"].shape[0]
    share = channels // n_dp
    chips = n_dp // 2
    images = n_dp * n_fsdp
    spread = share % 128 == 0
    dma = pltpu.SemaphoreType.DMA
    f32, half = jnp.float32, jnp.bfloat16
    shape = jax.ShapeDtypeStruct
    width = embed_width + 128
    piece = (channels + embed_width) // 8
    outs = dict(
        all_slope=(shape((n_dp, n_fsdp, rows, hid_width), half), ANY),
        gmat=(shape((images, channels), half), VMEM),
        row_down=(shape((images, hid_width), f32), VMEM),
        all_act=(shape((n_dp, n_fsdp, 1, hid_width), f32), VMEM),
        img_sum=(shape((pairs, embed_width), f32), VMEM),
        txt_sum=(shape((pairs, embed_width), f32), VMEM),
    )
    scratch = dict(
        up=pltpu.VMEM(w_up.shape, half),
        down=pltpu.VMEM(w_down.shape, half),
        proj=pltpu.VMEM(w_proj.shape, half),
        mixed=pltpu.VMEM((rows, channels), f32),
        norm=pltpu.VMEM((rows, channels), half),
        means=pltpu.VMEM((1, channels), f32),
        gimg=pltpu.VMEM((n_fsdp, pairs, width), half),
        ctxt=pltpu.VMEM((n_dp, pairs, width), half),
        slope=pltpu.VMEM((n_fsdp, rows, hid_width), half),
        all_grad=pltpu.VMEM((n_dp, n_fsdp, channels // 128, 128), half),
        gwide=pltpu.VMEM((images, channels // 128, 128), f32),
        grow=pltpu.VMEM((channels // 128, 128), f32),
        crit=pltpu.VMEM((n_fsdp, 8, piece), f32),
        crit_in=pltpu.VMEM((n_fsdp - 1, 8, piece), f32),
        lines=pltpu.VMEM((8, piece), f32),
        partial=pltpu.VMEM((n_fsdp, channels), f32),
        imgs=pltpu.VMEM((n_fsdp, pairs, embed_width), half),
        imgs_in=pltpu.VMEM((n_fsdp - 1, pairs, embed_width), half),
        txts=pltpu.VMEM((2, chips, pairs, embed_width), half),
        txts_pair=pltpu.VMEM((chips, pairs, embed_width), half),
        txts_sum=pltpu.VMEM((chips, pairs, embed_width), half),
        txts_in=pltpu.VMEM((chips - 1, pairs, embed_width), half),
    )
    if spread:
        outs.update(own=(shape((n_dp, n_fsdp, rows, share), half), ANY))
        scratch.update(grp=pltpu.VMEM((n_fsdp, rows, channels), half))
    else:
        outs.update(grp=(shape((n_fsdp, rows, channels), half), VMEM))
    sems = dict(
        loc=(4,),
        rgt=(n_fsdp,),
        lft=(n_fsdp,),
        col=(n_fsdp, n_dp - 1),
        slo=(n_fsdp, chips - 1),
        hlf=(n_fsdp, 2),
        par=(n_fsdp, chips),
        img=(n_fsdp - 1,),
        txt=(chips - 1,),
        txtp=(chips,),
        act=(chips - 1,),
        actp=(chips,),
        grd=(chips - 1,),
        grdp=(chips,),
        gra=(n_fsdp - 1,),
        cri=(n_fsdp - 1,),
        ims=(n_fsdp - 1,),
        txs=(chips - 1,),
        txx=(1,),
    )
    for name, dims in sems.items():
        if name == "loc":
            scratch[name] = dma(dims)
        else:
            scratch[name + "_s"] = dma(dims)
            scratch[name + "_r"] = dma(dims)
    scratch.update(col_l=dma((n_fsdp,)))
    scratch.update(slo_l=dma((n_fsdp,)))
    for name, one in args.items():
        scratch[name] = pltpu.VMEM(one.shape, one.dtype)
    scratch.update(first=dma((len(args),)))
    inputs = [name + "_hbm" for name in [*args, "up", "down", "proj"]]
    names = [*inputs, *outs, *scratch]
    results = pl.pallas_call(
        functools.partial(whole_kernel, n_dp, n_fsdp, spread, names, list(args)),
        out_shape=[one for one, _ in outs.values()],
        in_specs=[HBM] * (len(args) + 3),
        out_specs=[spec for _, spec in outs.values()],
        scratch_shapes=list(scratch.values()),
        compiler_params=pltpu.CompilerParams(
            collective_id=0, has_side_effects=True, vmem_limit_bytes=42 << 20
        ),
    )(*[pltpu.with_memory_space_constraint(one, pltpu.HBM) if one.size > 1 else one for one in [*args.values(), w_up, w_down, w_proj]])
    return types.SimpleNamespace(**dict(zip(outs, results)))


def finish_kernel(
    img_hbm, txt_hbm, img_sum, txt_sum, act, gmat, row_down, own, slopes,
    img_grad, txt_grad, up_hbm, down_hbm,
    img_emb, txt_emb, own_t, hid, up, downs, sems, out_sems,
):
    img_copy = pltpu.make_async_copy(img_hbm, img_emb, sems.at[0])
    txt_copy = pltpu.make_async_copy(txt_hbm, txt_emb, sems.at[1])
    img_copy.start()
    txt_copy.start()
    tiles, _, wide = up.shape
    all_rows = slopes.shape[0]
    images = gmat.shape[0]
    patches = all_rows // images
    share = own.shape[1]
    hid_width = tiles * wide
    d = lax.axis_index("dp")
    own_grad = gmat[:, pl.ds(pl.multiple_of(d * share, 128), share)]
    totals = jnp.concatenate([act[i] for i in range(images)], axis=0)
    high = totals.astype(jnp.bfloat16)
    low = (totals - high.astype(jnp.float32)).astype(jnp.bfloat16)
    both = jnp.concatenate([high, low], axis=0)
    grads = jnp.concatenate([own_grad, own_grad], axis=0)
    downs[...] = lax.dot_general(both, grads, (((0,), (0,)), ((), ())), preferred_element_type=jnp.float32)
    down_out = pltpu.make_async_copy(downs, down_hbm, out_sems.at[tiles])
    down_out.start()
    own_t[...] = own[...].T
    img_copy.wait()
    txt_copy.wait()
    for source, summed, result in ((img_emb, img_sum, img_grad), (txt_emb, txt_sum, txt_grad)):
        unit_part, length = unit_rows(source[...])
        result[...] = back_unit(summed[...], unit_part, length)

    def emit(i):
        return pltpu.make_async_copy(up.at[i], up_hbm.at[:, pl.ds(i * wide, wide)], out_sems.at[i])

    def weigh(i):
        for k in range(images):
            spot = pl.ds(k * patches, patches)
            factor = row_down[k : k + 1, i * wide : (i + 1) * wide]
            hid[i % 2, spot, :] = (slopes[spot, i * wide : (i + 1) * wide].astype(jnp.float32) * factor).astype(jnp.bfloat16)

    weigh(0)
    for i in range(tiles):
        if i + 1 < tiles:
            weigh(i + 1)
        up[i] = jnp.dot(own_t[...], hid[i % 2], preferred_element_type=jnp.float32)
        emit(i).start()
    down_out.wait()
    for i in range(tiles):
        emit(i).wait()


def run_finish(img_emb, txt_emb, got):
    n_dp, n_fsdp, rows, share = got.own.shape
    hid_width = got.row_down.shape[1]
    images, channels = got.gmat.shape
    all_rows = images * rows
    wide = 256 if hid_width % 256 == 0 else 128
    tiles = hid_width // wide
    f32, half = jnp.float32, jnp.bfloat16
    shape = jax.ShapeDtypeStruct
    return pl.pallas_call(
        finish_kernel,
        out_shape=(
            shape(img_emb.shape, f32),
            shape(txt_emb.shape, f32),
            shape((share, hid_width), f32),
            shape((hid_width, share), f32),
        ),
        in_specs=[HBM] * 2 + [VMEM] * 7,
        out_specs=(VMEM, VMEM, ANY, ANY),
        scratch_shapes=[
            pltpu.VMEM(img_emb.shape, half),
            pltpu.VMEM(txt_emb.shape, half),
            pltpu.VMEM((share, all_rows), half),
            pltpu.VMEM((2, all_rows, wide), half),
            pltpu.VMEM((tiles, share, wide), f32),
            pltpu.VMEM((hid_width, share), f32),
            pltpu.SemaphoreType.DMA((2,)),
            pltpu.SemaphoreType.DMA((tiles + 1,)),
        ],
        compiler_params=pltpu.CompilerParams(vmem_limit_bytes=24 << 20),
    )(
        pltpu.with_memory_space_constraint(img_emb, pltpu.HBM),
        pltpu.with_memory_space_constraint(txt_emb, pltpu.HBM),
        got.img_sum,
        got.txt_sum,
        got.all_act.reshape(images, 1, hid_width),
        got.gmat,
        got.row_down,
        got.own.reshape(all_rows, share),
        got.all_slope.reshape(all_rows, hid_width),
    )


def split_two(values):
    high = lax.reduce_precision(values, 8, 7)
    low = values - high
    return high.astype(jnp.bfloat16), low.astype(jnp.bfloat16)


def on_device(
    img_emb,
    txt_emb,
    img_ids,
    txt_ids,
    temp_log,
    logit_bias,
    block_in,
    dw_kernel,
    ln_gain,
    ln_bias,
    w_up,
    w_down,
    layer_scale,
    head_gain,
    head_bias,
    w_proj,
):
    rows, channels = block_in.shape
    hid_width = w_up.shape[1]
    n_dp, n_fsdp = lax.axis_size("dp"), lax.axis_size("fsdp")
    args = dict(
        block=block_in,
        kernel=dw_kernel,
        ln_gain=ln_gain[None],
        ln_bias=ln_bias[None],
        img_emb=img_emb,
        txt_emb=txt_emb,
        img_ids=img_ids[None],
        txt_ids=txt_ids[None],
        temper=temp_log.reshape(1, 1),
        offset=logit_bias.reshape(1, 1),
        scale=layer_scale[None],
        gain=head_gain[None],
        bias=head_bias[None],
    )
    got = run_whole(n_dp, n_fsdp, args, w_up, w_down, w_proj)
    share = channels // n_dp
    if share % 128 == 0:
        return run_finish(img_emb, txt_emb, got)
    own_normed = lax.all_to_all(got.grp.reshape(-1, channels), "dp", split_axis=1, concat_axis=0, tiled=True)
    slopes = got.all_slope.reshape(n_dp * n_fsdp, rows, hid_width).astype(jnp.float32)
    hid_grad = (slopes * got.row_down[:, None, :]).astype(jnp.bfloat16).reshape(-1, hid_width)
    w_up_grad = lax.dot_general(
        own_normed, hid_grad, (((0,), (0,)), ((), ())), preferred_element_type=jnp.float32
    )
    own_grad = lax.dynamic_slice_in_dim(got.gmat, lax.axis_index("dp") * share, share, 1)
    high, low = split_two(got.all_act.reshape(n_dp * n_fsdp, hid_width))
    w_down_grad = lax.dot_general(
        jnp.concatenate([high, low]),
        jnp.concatenate([own_grad, own_grad]),
        (((0,), (0,)), ((), ())),
        preferred_element_type=jnp.float32,
    )
    img_unit, img_len = unit_rows(img_emb)
    txt_unit, txt_len = unit_rows(txt_emb)
    img_grad = back_unit(got.img_sum, img_unit, img_len)
    txt_grad = back_unit(got.txt_sum, txt_unit, txt_len)
    return (img_grad, txt_grad, w_up_grad, w_down_grad)


def solution(mesh):
    in_specs = (
        P(("dp", "fsdp"), None),
        P(("dp", "fsdp"), None),
        P(("dp", "fsdp")),
        P(("dp", "fsdp")),
        P(),
        P(),
        P(("dp", "fsdp"), None),
        P(),
        P(),
        P(),
        P(None, "fsdp"),
        P("fsdp", None),
        P(),
        P(),
        P(),
        P(),
    )
    out_specs = (P(("dp", "fsdp"), None), P(("dp", "fsdp"), None), P("dp", "fsdp"), P("fsdp", "dp"))
    return jax.shard_map(
        on_device, mesh=mesh, in_specs=in_specs, out_specs=out_specs, check_vma=False
    )
```
